512 devices in a mesh: leaf: 8 (over x, core), front: 64 (over y, z).
Axes of the slice: x: 4, y: 8, z: 8, core: 2. Of those that a mesh axis runs over, the one named last changes fastest.
Arguments:
- rhs_leaf: float32 [8, 32, 229376], P('leaf', None, 'front'), may hold values from -6 to 6
- rhs_sep: float32 [8, 32, 8192], P('leaf', None, 'front'), may hold values from -6 to 6
- leaf_inv: float32 [8, 1792, 128, 128], P('leaf', 'front')
- leaf_update: float32 [8, 1792, 128, 128], P('leaf', 'front'), may hold values from -0.09375 to 0.09375
- update_rows: int32 [8, 1792, 128], P('leaf', 'front'), may hold values from 0 to 128, as said below
- update_owner: int32 [8, 1792, 1], P('leaf', 'front'), may hold values from 0 to 63; in each aligned block of 28 rows (0 to 27, 28 to 55, ..., all dimensions but the last counted through in order) no two rows name the same one
- sep_inv: float32 [8, 64, 128, 128], P('leaf', 'front')
- sep_couple: float32 [8, 64, 128, 128], P('leaf', 'front'), may hold values from -0.375 to 0.375
Outputs:
- x_leaf: float32 [8, 32, 229376], P('leaf', None, 'front')
- x_sep: float32 [8, 32, 8192], P('leaf', None, 'front')
The draws below stay inside these ranges and needn't reach their ends.
Inputs may be any that keep to these rules, and one draw needn't show every extreme that they name: `update_rows`: within each leaf front the entries below 128 are distinct; the entries equal to 128 mark padded rows and come last in the front; some front has 64 padded rows. `update_owner`: at most 1 of the 28 leaf fronts held by one index of front have the same owner, and some index of front reaches 1.
All inputs are finite; a program needn't handle non-finite values.
Results may differ from the reference program's by a relative error of at most 0.0001.
Values sent between devices are 32-bit elements; how exact they have to be, the bound alone decides.
No kernel may reach another device: no remote copies, remote signals or barrier semaphores. Data moves between devices by JAX's collectives and lax.ppermute only.
A program may use at most 64 MiB of HBM per device.

```python
import math
import jax
import jax.numpy as jnp
import numpy as np
from jax import lax

P_SIZE = 128
R = 32
LF = 28
CAP = 1
GROUPS = 8
FRONTS = 1792
LEAF_ROWS = 229376
SEP_ROWS = 8192
N_FRONT = 64


def inverse_blocks(key, shape):
    noise = jnp.clip(jax.random.normal(key, shape, jnp.float32), -4.0, 4.0)
    return jnp.eye(P_SIZE, dtype=jnp.float32) + 0.5 / math.sqrt(P_SIZE) * noise


def draw_leaf_inv(key, part):
    return inverse_blocks(jax.random.fold_in(key, 11), (GROUPS, FRONTS, P_SIZE, P_SIZE))


def draw_sep_inv(key, part):
    return inverse_blocks(jax.random.fold_in(key, 13), (GROUPS, SEP_ROWS // P_SIZE, P_SIZE, P_SIZE))


def draw_update_rows(key, part):
    total = GROUPS * FRONTS
    keys = jax.random.split(jax.random.fold_in(key, 17), total)
    shuffled = jax.vmap(lambda k: jax.random.permutation(k, P_SIZE))(keys).astype(jnp.int32)
    live_count = jax.random.randint(jax.random.fold_in(key, 19), (total, 1), P_SIZE // 2, P_SIZE + 1).astype(jnp.int32)
    live_count = live_count.at[0, 0].set(P_SIZE // 2)
    positions = jnp.arange(P_SIZE, dtype=jnp.int32)[None, :]
    result = jnp.where(positions < live_count, shuffled, P_SIZE)
    return result.reshape(GROUPS, FRONTS, P_SIZE).astype(jnp.int32)


def block_scale(stream_key, dims, shards, least, largest):
    level, own = 1.0, jax.random.fold_in(stream_key, 6)
    for dim, parts in shards:
        draws = jnp.exp(jax.random.uniform(jax.random.fold_in(own, dim), (parts,), jnp.float32, least / len(shards), largest / len(shards)))
        level = level * jnp.repeat(draws, dims[dim] // parts).reshape([-1 if axis == dim else 1 for axis in range(len(dims))])
    return level


def routed_block(own_key, own, number, rows, amount, top, limit, lean):
    ranking = jax.random.permutation(own_key, amount)
    packed, usual = portions_of(amount, rows * top, limit, lean, True), portions_of(amount, rows * top, limit, lean, False)
    places = jnp.arange(amount)

    def named(sizes, offset_by):
        used = int((sizes > 0).sum())
        fixed = max(1, used // 4)
        shifted = fixed + (places - fixed + offset_by * (used - fixed)) % max(1, amount - fixed)
        return jnp.zeros((amount,), jnp.int32).at[ranking[jnp.where(places < fixed, places, shifted)]].set(jnp.asarray(sizes, jnp.int32))

    sizes = jnp.where(number % 4 == 0, named(packed, number // 4), named(usual, number - number // 4 - 1))
    mixed = jax.random.permutation(jax.random.fold_in(own, 3), amount)
    donor, sink = mixed[0:amount // 2 * 2:2], mixed[1:amount // 2 * 2:2]
    margin = jnp.minimum(sizes[donor] - 1, limit - sizes[sink]) // 2
    margin = jnp.where((donor == ranking[0]) | (sink == ranking[0]) | (sizes[sink] == 0), 0, jnp.maximum(margin, 0))
    shifted = jax.random.randint(jax.random.fold_in(own, 4), (amount // 2,), 0, 1 << 20) % (margin + 1)
    sizes = sizes.at[donor].add(-shifted).at[sink].add(shifted)
    labels = jnp.searchsorted(jnp.cumsum(sizes), jnp.arange(rows * top), side="right").astype(jnp.int32)
    table = labels.reshape(top, rows).T
    table = table[jax.random.permutation(jax.random.fold_in(own, 1), rows)]
    offset_by = jax.random.randint(jax.random.fold_in(own, 2), (rows, 1), 0, top)
    return jnp.take_along_axis(table, (jnp.arange(top)[None, :] + offset_by) % top, axis=1)


def portions_of(count, total, reach, slope, full):
    loads = [(1 << 20) // math.isqrt(rank ** slope) + 1 for rank in range(1, count + 1)]
    largest = reach if full else min(reach, max(-(-total // count), total * loads[0] // sum(loads)))
    least = 1 if total - largest >= count - 1 else 0
    counts, surplus = [largest] + [least] * (count - 1), total - largest - least * (count - 1)
    while surplus > 0:
        free = [i for i in range(1, count) if counts[i] < largest] or [i for i in range(1, count) if counts[i] < reach]
        mass, budget = sum([loads[i] for i in free]), surplus
        for i in free:
            more = min(reach - counts[i], max(1, budget * loads[i] // mass), surplus)
            counts[i] = counts[i] + more
            surplus = surplus - more
    return np.array(counts)


def scatter_about(rng, extent, width, most, pieces=(), held_as=jnp.bfloat16):
    values = width * jax.random.normal(rng, extent, jnp.float32)
    if pieces:
        values = values * block_scale(rng, extent, pieces, -0.22, 0.18)
    return jnp.clip(values, -most, most).astype(held_as)


def setup_inputs(seed: int = 0) -> dict:
    arg_keys = jax.random.split(jax.random.key(seed), 9)
    rhs_leaf = scatter_about(arg_keys[0], (GROUPS, R, LEAF_ROWS), 1.0, 6.0, ((0, 8), (2, 64)), jnp.float32)
    rhs_sep = scatter_about(arg_keys[1], (GROUPS, R, SEP_ROWS), 1.0, 6.0, ((0, 8), (2, 64)), jnp.float32)
    leaf_inv = draw_leaf_inv(jax.random.fold_in(arg_keys[8], 71), 0)
    leaf_update = scatter_about(arg_keys[3], (GROUPS, FRONTS, P_SIZE, P_SIZE), (P_SIZE * LF) ** -0.5, 0.09375, ((0, 8), (1, 64)), jnp.float32)
    update_rows = draw_update_rows(jax.random.fold_in(arg_keys[8], 71), 0)
    update_owner_keys = jax.random.split(jax.random.fold_in(arg_keys[5], 1), GROUPS * FRONTS // LF)
    update_owner_turns = jax.random.permutation(jax.random.fold_in(arg_keys[5], 3), GROUPS * FRONTS // LF)
    update_owner = jax.vmap(lambda own, number: routed_block(jax.random.fold_in(arg_keys[5], 2), own, number, LF, N_FRONT, 1, CAP, 2))(update_owner_keys, update_owner_turns).reshape((GROUPS, FRONTS, 1))
    sep_inv = draw_sep_inv(jax.random.fold_in(arg_keys[8], 71), 0)
    sep_couple = scatter_about(arg_keys[7], (GROUPS, N_FRONT, P_SIZE, P_SIZE), (2 * P_SIZE) ** -0.5, 0.375, ((0, 8), (1, 64)), jnp.float32)
    return {"rhs_leaf": rhs_leaf, "rhs_sep": rhs_sep, "leaf_inv": leaf_inv, "leaf_update": leaf_update, "update_rows": update_rows, "update_owner": update_owner, "sep_inv": sep_inv, "sep_couple": sep_couple}


def apply_blocks(matrices, vectors):
    return jnp.einsum('bik,rbk->rbi', matrices, vectors, precision=lax.Precision.HIGHEST)


def apply_transposed(matrices, vectors):
    return jnp.einsum('bki,rbk->rbi', matrices, vectors, precision=lax.Precision.HIGHEST)


def collect_group(updates, targets):
    flat = updates.reshape(updates.shape[0], -1)
    return jnp.zeros((updates.shape[0], SEP_ROWS), updates.dtype).at[:, targets.reshape(-1)].add(flat)


def pick_group(solution, targets):
    return jnp.take(solution, targets.reshape(-1), axis=1).reshape(solution.shape[0], FRONTS, P_SIZE)


def reference(rhs_leaf, rhs_sep, leaf_inv, leaf_update, update_rows, update_owner, sep_inv, sep_couple):
    highest = lax.Precision.HIGHEST
    right_leaf = rhs_leaf.reshape(GROUPS, R, FRONTS, P_SIZE)
    leaf_y = jnp.einsum('gfik,grfk->grfi', leaf_inv, right_leaf, precision=highest)
    updates = jnp.einsum('gfik,grfk->grfi', leaf_update, leaf_y, precision=highest)
    live_mask = update_rows < P_SIZE
    targets = (update_owner * P_SIZE + jnp.minimum(update_rows, P_SIZE - 1)).astype(jnp.int32)
    updates = jnp.where(live_mask[:, None], updates, 0.0)
    collected = jax.vmap(collect_group)(updates, targets)
    reduced = (rhs_sep - collected).reshape(GROUPS, R, N_FRONT, P_SIZE)
    forward = []
    previous = jnp.zeros((R, N_FRONT, P_SIZE), reduced.dtype)
    for group in range(GROUPS):
        current = apply_blocks(sep_inv[group], reduced[group] - apply_blocks(sep_couple[group], previous))
        forward.append(current)
        previous = current
    backward = [None] * GROUPS
    following = jnp.zeros((R, N_FRONT, P_SIZE), reduced.dtype)
    for group in range(GROUPS - 1, -1, -1):
        if group < GROUPS - 1:
            residue = forward[group] - apply_transposed(sep_couple[group + 1], following)
        else:
            residue = forward[group]
        current = apply_transposed(sep_inv[group], residue)
        backward[group] = current
        following = current
    x_sep = jnp.stack(backward).reshape(GROUPS, R, SEP_ROWS)
    picked = jax.vmap(pick_group)(x_sep, targets)
    picked = jnp.where(live_mask[:, None], picked, 0.0)
    residue = leaf_y - jnp.einsum('gfki,grfk->grfi', leaf_update, picked, precision=highest)
    x_leaf = jnp.einsum('gfki,grfk->grfi', leaf_inv, residue, precision=highest)
    return x_leaf.reshape(GROUPS, R, LEAF_ROWS), x_sep
```

```python
import jax
import jax.numpy as jnp
from jax import lax
from jax.experimental import pallas as pl
from jax.experimental.pallas import tpu as pltpu
from jax.sharding import PartitionSpec as P

NT = (((1,), (1,)), ((), ()))
NN = (((1,), (0,)), ((), ()))


def split(value):
    high = value.astype(jnp.bfloat16)
    low = (value - high.astype(jnp.float32)).astype(jnp.bfloat16)
    return high, low


def product(left, right, dims):
    rows = left.shape[0]
    left_high, left_low = split(left)
    right_high, right_low = split(right)
    both = lax.dot_general(
        jnp.concatenate([left_high, left_low], axis=0), right_high, dims, preferred_element_type=jnp.float32
    )
    cross = lax.dot_general(left_high, right_low, dims, preferred_element_type=jnp.float32)
    return both[:rows] + (both[rows:] + cross)


def select(left, chosen, dims):
    rows = left.shape[0]
    both = lax.dot_general(
        jnp.concatenate(split(left), axis=0), chosen, dims, preferred_element_type=jnp.float32
    )
    return both[:rows] + both[rows:]


def chosen_rows(row_index, block_rows):
    separator_row = lax.broadcasted_iota(jnp.int32, (block_rows, block_rows), 0)
    return jnp.where(separator_row == row_index, 1.0, 0.0).astype(jnp.bfloat16)


def leaf_forward(owner_ref, rhs_ref, inv_ref, update_ref, rows_ref, y_ref, dense_ref):
    step = pl.program_id(0)
    count, block_rows, _ = inv_ref.shape

    @pl.when(step == 0)
    def _():
        dense_ref[...] = jnp.zeros_like(dense_ref)

    for front in range(count):
        right = rhs_ref[:, front * block_rows : (front + 1) * block_rows]
        leaf_y = product(right, inv_ref[front], NT)
        y_ref[front] = leaf_y
        update = product(leaf_y, update_ref[front], NT)
        placed = select(update, chosen_rows(rows_ref[front], block_rows), NT)
        dense_ref[owner_ref[step * count + front]] = placed


def leaf_backward(owner_ref, x_ref, y_ref, inv_ref, update_ref, rows_ref, out_ref):
    step = pl.program_id(0)
    count, block_rows, _ = inv_ref.shape
    for front in range(count):
        owned = x_ref[owner_ref[step * count + front]]
        picked = select(owned, chosen_rows(rows_ref[front], block_rows), NN)
        residue = y_ref[front] - product(picked, update_ref[front], NN)
        out_ref[:, front * block_rows : (front + 1) * block_rows] = product(residue, inv_ref[front], NN)


def chain(group_ref, reduced_ref, blocks_ref, x_ref, y_scratch, x_scratch):
    groups = reduced_ref.shape[0]
    for group in range(groups):
        right = reduced_ref[group]
        if group:
            right = right - product(y_scratch[group - 1], blocks_ref[group, 1], NT)
        y_scratch[group] = product(right, blocks_ref[group, 0], NT)
    for group in range(groups - 1, -1, -1):
        right = y_scratch[group]
        if group < groups - 1:
            right = right - product(x_scratch[group + 1], blocks_ref[group + 1, 1], NN)
        x_scratch[group] = product(right, blocks_ref[group, 0], NN)
    x_ref[...] = x_scratch[group_ref[0]]


PER_STEP = 7
VMEM = pl.BlockSpec(memory_space=pltpu.VMEM)
SMEM = pl.BlockSpec(memory_space=pltpu.SMEM)
PARAMS = pltpu.CompilerParams(vmem_limit_bytes=32 << 20)


def per_device(
    rhs_leaf, rhs_sep, leaf_inv, leaf_update, update_rows, update_owner, sep_inv, sep_couple
):
    front_count, block_rows = leaf_inv.shape[1], leaf_inv.shape[3]
    rhs_count = rhs_leaf.shape[1]
    groups = lax.axis_size("leaf")
    fronts = lax.axis_size("front")
    right_leaf, inverse, coupling = rhs_leaf[0], leaf_inv[0], leaf_update[0]
    rows = update_rows.reshape(front_count, 1, block_rows)
    owners = update_owner.reshape(front_count)

    blocks = jnp.concatenate([sep_inv, sep_couple], axis=1)
    blocks = lax.all_gather(blocks, "leaf", axis=0, tiled=True)

    matrices = pl.BlockSpec((PER_STEP, block_rows, block_rows), lambda s: (s, 0, 0))
    lines = pl.BlockSpec((PER_STEP, 1, block_rows), lambda s: (s, 0, 0))
    vectors = pl.BlockSpec((PER_STEP, rhs_count, block_rows), lambda s: (s, 0, 0))
    columns = pl.BlockSpec((rhs_count, PER_STEP * block_rows), lambda s: (0, s))
    whole = pl.BlockSpec((fronts, rhs_count, block_rows), lambda s: (0, 0, 0))
    leaf_y, dense = pl.pallas_call(
        leaf_forward,
        grid=(front_count // PER_STEP,),
        in_specs=[SMEM, columns, matrices, matrices, lines],
        out_specs=[vectors, whole],
        out_shape=[
            jax.ShapeDtypeStruct((front_count, rhs_count, block_rows), jnp.float32),
            jax.ShapeDtypeStruct((fronts, rhs_count, block_rows), jnp.float32),
        ],
        compiler_params=PARAMS,
        name="leaf_forward",
    )(owners, right_leaf, inverse, coupling, rows)

    received = lax.all_to_all(dense, "front", 0, 0, tiled=True)
    reduced = rhs_sep[0] - jnp.sum(received, axis=0)
    reduced = lax.all_gather(reduced, "leaf", axis=0)
    x_sep = pl.pallas_call(
        chain,
        in_specs=[SMEM, VMEM, VMEM],
        out_specs=VMEM,
        out_shape=jax.ShapeDtypeStruct((rhs_count, block_rows), jnp.float32),
        scratch_shapes=[
            pltpu.VMEM((groups, rhs_count, block_rows), jnp.float32),
            pltpu.VMEM((groups, rhs_count, block_rows), jnp.float32),
        ],
        compiler_params=PARAMS,
        name="chain",
    )(lax.axis_index("leaf").reshape(1), reduced, blocks)

    copies = jnp.broadcast_to(x_sep[None], (fronts, rhs_count, block_rows))
    gathered = lax.all_to_all(copies, "front", 0, 0, tiled=True)
    x_leaf = pl.pallas_call(
        leaf_backward,
        grid=(front_count // PER_STEP,),
        in_specs=[SMEM, whole, vectors, matrices, matrices, lines],
        out_specs=columns,
        out_shape=jax.ShapeDtypeStruct((rhs_count, front_count * block_rows), jnp.float32),
        compiler_params=PARAMS,
        name="leaf_backward",
    )(owners, gathered, leaf_y, inverse, coupling, rows)
    return (x_leaf[None], x_sep[None])


def solution(mesh):
    placed = (
        P("leaf", None, "front"),
        P("leaf", None, "front"),
        P("leaf", "front", None, None),
        P("leaf", "front", None, None),
        P("leaf", "front", None),
        P("leaf", "front", None),
        P("leaf", "front", None, None),
        P("leaf", "front", None, None),
    )
    return jax.shard_map(
        per_device,
        mesh=mesh,
        in_specs=placed,
        out_specs=(P("leaf", None, "front"), P("leaf", None, "front")),
        check_vma=False,
    )
```

```python
import jax
import jax.numpy as jnp
from jax import lax
from jax.experimental import pallas as pl
from jax.experimental.pallas import tpu as pltpu
from jax.sharding import PartitionSpec as P

NT = (((1,), (1,)), ((), ()))
NN = (((1,), (0,)), ((), ()))


def split(value):
    high = value.astype(jnp.bfloat16)
    low = (value - high.astype(jnp.float32)).astype(jnp.bfloat16)
    return high, low


def product(left, right, dims):
    rows = left.shape[0]
    left_high, left_low = split(left)
    right_high, right_low = split(right)
    both = lax.dot_general(
        jnp.concatenate([left_high, left_low], axis=0), right_high, dims, preferred_element_type=jnp.float32
    )
    cross = lax.dot_general(left_high, right_low, dims, preferred_element_type=jnp.float32)
    return both[:rows] + (both[rows:] + cross)


def select(left, chosen, dims):
    rows = left.shape[0]
    both = lax.dot_general(
        jnp.concatenate(split(left), axis=0), chosen, dims, preferred_element_type=jnp.float32
    )
    return both[:rows] + both[rows:]


def chosen_rows(row_index, block_rows):
    separator_row = lax.broadcasted_iota(jnp.int32, (block_rows, block_rows), 0)
    return jnp.where(separator_row == row_index, 1.0, 0.0).astype(jnp.bfloat16)


def coupled_inverse(inv_ref, couple_ref, out_ref):
    coupled = product(inv_ref[...], couple_ref[...], NN)
    for copy in range(out_ref.shape[0]):
        out_ref[copy] = coupled


def leaf_forward(owner_ref, rhs_ref, inv_ref, update_ref, rows_ref, y_ref, dense_ref):
    step = pl.program_id(0)
    count, block_rows, _ = inv_ref.shape

    @pl.when(step == 0)
    def _():
        dense_ref[...] = jnp.zeros_like(dense_ref)

    for front in range(count):
        right = rhs_ref[:, front * block_rows : (front + 1) * block_rows]
        leaf_y = product(right, inv_ref[front], NT)
        y_ref[front] = leaf_y
        update = product(leaf_y, update_ref[front], NT)
        placed = select(update, chosen_rows(rows_ref[front], block_rows), NT)
        dense_ref[owner_ref[step * count + front]] = placed


def leaf_prepare(y_ref, inv_ref, update_ref, rows_ref, own_ref, high_ref, low_ref):
    count, block_rows, _ = inv_ref.shape
    for front in range(count):
        inverse = inv_ref[front]
        own_ref[front] = product(y_ref[front], inverse, NN)
        mapped_high, mapped_low = split(product(update_ref[front], inverse, NN))
        chosen = chosen_rows(rows_ref[front], block_rows)
        placed = lax.dot_general(chosen, mapped_high, NN, preferred_element_type=jnp.float32)
        placed = placed + lax.dot_general(chosen, mapped_low, NN, preferred_element_type=jnp.float32)
        high_ref[front], low_ref[front] = split(placed)


def reduce_right(received_ref, rhs_ref, inv_ref, out_ref):
    reduced = rhs_ref[...] - jnp.sum(received_ref[...], axis=0)
    solved = product(reduced, inv_ref[...], NT)
    for copy in range(out_ref.shape[0]):
        out_ref[copy] = solved


def chain(group_ref, right_ref, coupled_ref, inv_ref, x_ref, copies_ref, scratch):
    groups = right_ref.shape[0]
    scratch[0] = right_ref[0]
    for group in range(1, groups):
        scratch[group] = right_ref[group] - product(scratch[group - 1], coupled_ref[group], NT)
    for group in range(groups - 1, 0, -1):
        scratch[group - 1] = scratch[group - 1] - product(scratch[group], coupled_ref[group], NN)
    x_sep = product(scratch[group_ref[0]], inv_ref[...], NN)
    x_ref[...] = x_sep
    for copy in range(copies_ref.shape[0]):
        copies_ref[copy] = x_sep


def leaf_backward(owner_ref, x_ref, own_ref, high_ref, low_ref, out_ref):
    count, rows, block_rows = own_ref.shape
    for front in range(count):
        owned_high, owned_low = split(x_ref[owner_ref[front]])
        both = lax.dot_general(
            jnp.concatenate([owned_high, owned_low], axis=0),
            high_ref[front],
            NN,
            preferred_element_type=jnp.float32,
        )
        cross = lax.dot_general(owned_high, low_ref[front], NN, preferred_element_type=jnp.float32)
        mapped = both[:rows] + (both[rows:] + cross)
        out_ref[:, front * block_rows : (front + 1) * block_rows] = own_ref[front] - mapped


PER_STEP = 7
VMEM = pl.BlockSpec(memory_space=pltpu.VMEM)
SMEM = pl.BlockSpec(memory_space=pltpu.SMEM)
PARAMS = pltpu.CompilerParams(vmem_limit_bytes=32 << 20)


def floats(*shape):
    return jax.ShapeDtypeStruct(shape, jnp.float32)


def call(body, in_specs, out_specs, out_shape, **rest):
    return pl.pallas_call(
        body,
        in_specs=in_specs,
        out_specs=out_specs,
        out_shape=out_shape,
        compiler_params=PARAMS,
        name=body.__name__,
        **rest,
    )


def per_device(
    rhs_leaf, rhs_sep, leaf_inv, leaf_update, update_rows, update_owner, sep_inv, sep_couple
):
    front_count, size = leaf_inv.shape[1], leaf_inv.shape[3]
    width = rhs_leaf.shape[1]
    groups = lax.axis_size("leaf")
    fronts = lax.axis_size("front")
    right_leaf = rhs_leaf[0]
    inverse = pltpu.with_memory_space_constraint(leaf_inv[0], pltpu.HBM)
    coupling = pltpu.with_memory_space_constraint(leaf_update[0], pltpu.HBM)
    rows = update_rows.reshape(front_count, 1, size)
    owners = update_owner.reshape(front_count)
    separator_inverse, separator_couple = sep_inv[0, 0], sep_couple[0, 0]

    matrices = pl.BlockSpec((PER_STEP, size, size), lambda s: (s, 0, 0))
    lines = pl.BlockSpec((PER_STEP, 1, size), lambda s: (s, 0, 0))
    vectors = pl.BlockSpec((PER_STEP, width, size), lambda s: (s, 0, 0))
    columns = pl.BlockSpec((width, PER_STEP * size), lambda s: (0, s))
    whole = pl.BlockSpec((fronts, width, size), lambda s: (0, 0, 0))
    steps = (front_count // PER_STEP,)

    coupled = call(coupled_inverse, [VMEM, VMEM], VMEM, floats(groups, size, size))(
        separator_inverse, separator_couple
    )
    coupled = lax.all_to_all(coupled, "leaf", 0, 0, tiled=True)

    leaf_y, dense = call(
        leaf_forward,
        [SMEM, columns, matrices, matrices, lines],
        [vectors, whole],
        [floats(front_count, width, size), floats(fronts, width, size)],
        grid=steps,
    )(owners, right_leaf, inverse, coupling, rows)
    dense, coupled = lax.optimization_barrier((dense, coupled))
    received = lax.all_to_all(dense, "front", 0, 0, tiled=True)
    halves = jax.ShapeDtypeStruct((front_count, size, size), jnp.bfloat16)
    own, high, low = call(
        leaf_prepare,
        [vectors, matrices, matrices, lines],
        [vectors, matrices, matrices],
        [floats(front_count, width, size), halves, halves],
        grid=steps,
    )(leaf_y, inverse, coupling, rows)

    right = call(reduce_right, [VMEM, VMEM, VMEM], VMEM, floats(groups, width, size))(
        received, rhs_sep[0], separator_inverse
    )
    right = lax.all_to_all(right, "leaf", 0, 0, tiled=True)
    x_sep, copies = call(
        chain,
        [SMEM, VMEM, VMEM, VMEM],
        [VMEM, VMEM],
        [floats(width, size), floats(fronts, width, size)],
        scratch_shapes=[pltpu.VMEM((groups, width, size), jnp.float32)],
    )(lax.axis_index("leaf").reshape(1), right, coupled, separator_inverse)
    gathered = lax.all_to_all(copies, "front", 0, 0, tiled=True)
    x_leaf = call(
        leaf_backward, [SMEM, VMEM, VMEM, VMEM, VMEM], VMEM, floats(width, front_count * size)
    )(owners, gathered, own, high, low)
    return (x_leaf[None], x_sep[None])


def solution(mesh):
    placed = (
        P("leaf", None, "front"),
        P("leaf", None, "front"),
        P("leaf", "front", None, None),
        P("leaf", "front", None, None),
        P("leaf", "front", None),
        P("leaf", "front", None),
        P("leaf", "front", None, None),
        P("leaf", "front", None, None),
    )
    return jax.shard_map(
        per_device,
        mesh=mesh,
        in_specs=placed,
        out_specs=(P("leaf", None, "front"), P("leaf", None, "front")),
        check_vma=False,
    )
```

```python
import jax
import jax.numpy as jnp
from jax import lax
from jax.experimental import pallas as pl
from jax.experimental.pallas import tpu as pltpu
from jax.sharding import PartitionSpec as P

NT = (((1,), (1,)), ((), ()))
NN = (((1,), (0,)), ((), ()))


def dot(left, right, dims):
    return lax.dot_general(left, right, dims, preferred_element_type=jnp.float32)


def split(value):
    high = value.astype(jnp.bfloat16)
    low = (value - high.astype(jnp.float32)).astype(jnp.bfloat16)
    return high, low


def three_parts(parts, rows, size):
    return parts[:rows, :size] + (parts[rows:, :size] + parts[:rows, size:])


def product(left, right, dims):
    along = 0 if dims is NT else 1
    parts = dot(jnp.concatenate(split(left), axis=0), jnp.concatenate(split(right), axis=along), dims)
    return three_parts(parts, left.shape[0], right.shape[0])


def select(left, chosen, dims):
    rows = left.shape[0]
    both = dot(jnp.concatenate(split(left), axis=0), chosen, dims)
    return both[:rows] + both[rows:]


def chosen_rows(row_index, block_rows):
    separator_row = lax.broadcasted_iota(jnp.int32, (block_rows, block_rows), 0)
    return jnp.where(separator_row == row_index, 1.0, 0.0).astype(jnp.bfloat16)


def leaf_forward(owner_ref, rhs_ref, inv_ref, update_ref, rows_ref, y_ref, dense_ref):
    step = pl.program_id(0)
    count, size, _ = inv_ref.shape

    @pl.when(step == 0)
    def _():
        dense_ref[...] = jnp.zeros_like(dense_ref)

    leaf_y = [product(rhs_ref[:, f * size : (f + 1) * size], inv_ref[f], NT) for f in range(count)]
    for f in range(count):
        y_ref[f] = leaf_y[f]
    updates = [product(leaf_y[f], update_ref[f], NT) for f in range(count)]
    placed = [select(updates[f], chosen_rows(rows_ref[f], size), NT) for f in range(count)]
    for f in range(count):
        dense_ref[owner_ref[step * count + f]] = placed[f]


def coupled_inverse(inv_ref, couple_ref, after_ref, out_ref):
    out_ref[0] = product(inv_ref[...], couple_ref[...], NN)


def leaf_prepare(y_ref, inv_ref, update_ref, rows_ref, own_ref, mapped_ref):
    count, size, _ = inv_ref.shape
    for f in range(count):
        inverse = inv_ref[f]
        own_ref[:, f * size : (f + 1) * size] = product(y_ref[f], inverse, NN)
        mapped = jnp.concatenate(split(product(update_ref[f], inverse, NN)), axis=1)
        placed = dot(chosen_rows(rows_ref[f], size), mapped, NN)
        mapped_ref[f] = jnp.concatenate(split(placed[:, :size] + placed[:, size:]), axis=1)


def reduce_right(received_ref, rhs_ref, inv_ref, out_ref):
    reduced = rhs_ref[...] - jnp.sum(received_ref[...], axis=0)
    solved = product(reduced, inv_ref[...], NT)
    for copy in range(out_ref.shape[0]):
        out_ref[copy] = solved


def chain(group_ref, right_ref, coupled_ref, inv_ref, x_ref, copies_ref, scratch):
    groups = right_ref.shape[0]
    own = group_ref[0]
    solved = [right_ref[0]]
    for group in range(1, groups):
        coupled = coupled_ref[jnp.bitwise_xor(own, group)]
        solved.append(right_ref[group] - product(solved[-1], coupled, NT))
    residue = solved[-1]
    scratch[groups - 1] = residue
    for group in range(groups - 1, 0, -1):
        coupled = coupled_ref[jnp.bitwise_xor(own, group)]
        residue = solved[group - 1] - product(residue, coupled, NN)
        scratch[group - 1] = residue
    x_sep = product(scratch[own], inv_ref[...], NN)
    x_ref[...] = x_sep
    for copy in range(copies_ref.shape[0]):
        copies_ref[copy] = x_sep


def leaf_backward(owner_ref, x_ref, own_hbm, mapped_ref, out_ref, own_ref, arrived):
    count, size, _ = mapped_ref.shape
    rows = out_ref.shape[0]
    fetch = pltpu.make_async_copy(own_hbm, own_ref, arrived)
    fetch.start()
    for f in range(count):
        owned = jnp.concatenate(split(x_ref[owner_ref[f]]), axis=0)
        out_ref[:, f * size : (f + 1) * size] = three_parts(dot(owned, mapped_ref[f], NN), rows, size)
    fetch.wait()
    out_ref[...] = own_ref[...] - out_ref[...]


FORWARD_STEP = 14
PREPARE_STEP = 7
VMEM = pl.BlockSpec(memory_space=pltpu.VMEM)
SMEM = pl.BlockSpec(memory_space=pltpu.SMEM)
ANY = pl.BlockSpec(memory_space=pl.ANY)
PARAMS = pltpu.CompilerParams(vmem_limit_bytes=32 << 20)


def floats(*shape):
    return jax.ShapeDtypeStruct(shape, jnp.float32)


def call(body, in_specs, out_specs, out_shape, **rest):
    return pl.pallas_call(
        body,
        in_specs=in_specs,
        out_specs=out_specs,
        out_shape=out_shape,
        compiler_params=PARAMS,
        name=body.__name__,
        **rest,
    )


def gather_by_bits(value, axis):
    count, bit = lax.axis_size(axis), 1
    while bit < count:
        pairs = [(source, source ^ bit) for source in range(count)]
        value = jnp.concatenate([value, lax.ppermute(value, axis, pairs)], axis=0)
        bit *= 2
    return value


def per_device(
    rhs_leaf, rhs_sep, leaf_inv, leaf_update, update_rows, update_owner, sep_inv, sep_couple
):
    front_count, size = leaf_inv.shape[1], leaf_inv.shape[3]
    width = rhs_leaf.shape[1]
    groups = lax.axis_size("leaf")
    fronts = lax.axis_size("front")

    def stay(value):
        return pltpu.with_memory_space_constraint(value, pltpu.HBM)

    right_leaf, inverse, coupling = stay(rhs_leaf[0]), stay(leaf_inv[0]), stay(leaf_update[0])
    rows = stay(update_rows.reshape(front_count, 1, size))
    owners = stay(update_owner.reshape(front_count))
    separator_inverse, separator_couple = sep_inv[0, 0], sep_couple[0, 0]

    def specs(step):
        matrices = pl.BlockSpec((step, size, size), lambda s: (s, 0, 0))
        lines = pl.BlockSpec((step, 1, size), lambda s: (s, 0, 0))
        vectors = pl.BlockSpec((step, width, size), lambda s: (s, 0, 0))
        columns = pl.BlockSpec((width, step * size), lambda s: (0, s))
        return matrices, lines, vectors, columns

    matrices, lines, vectors, columns = specs(FORWARD_STEP)
    whole = pl.BlockSpec((fronts, width, size), lambda s: (0, 0, 0))
    leaf_y, dense = call(
        leaf_forward,
        [SMEM, columns, matrices, matrices, lines],
        [vectors, whole],
        [floats(front_count, width, size), floats(fronts, width, size)],
        grid=(front_count // FORWARD_STEP,),
    )(owners, right_leaf, inverse, coupling, rows)
    received = lax.all_to_all(dense, "front", 0, 0, tiled=True)

    coupled = call(coupled_inverse, [VMEM, VMEM, ANY], VMEM, floats(1, size, size))(
        separator_inverse, separator_couple, leaf_y
    )
    coupled = gather_by_bits(coupled, "leaf")
    matrices, lines, vectors, columns = specs(PREPARE_STEP)
    own, mapped = call(
        leaf_prepare,
        [vectors, matrices, matrices, lines],
        [columns, pl.BlockSpec((PREPARE_STEP, size, 2 * size), lambda s: (s, 0, 0))],
        [
            floats(width, front_count * size),
            jax.ShapeDtypeStruct((front_count, size, 2 * size), jnp.bfloat16),
        ],
        grid=(front_count // PREPARE_STEP,),
    )(leaf_y, inverse, coupling, rows)

    own = stay(own)
    right = call(reduce_right, [VMEM, VMEM, VMEM], VMEM, floats(groups, width, size))(
        received, rhs_sep[0], separator_inverse
    )
    right = lax.all_to_all(right, "leaf", 0, 0, tiled=True)
    x_sep, copies = call(
        chain,
        [SMEM, VMEM, VMEM, VMEM],
        [VMEM, VMEM],
        [floats(width, size), floats(fronts, width, size)],
        scratch_shapes=[pltpu.VMEM((groups, width, size), jnp.float32)],
    )(lax.axis_index("leaf").reshape(1), right, coupled, separator_inverse)
    gathered = lax.all_to_all(copies, "front", 0, 0, tiled=True)
    x_leaf = call(
        leaf_backward,
        [SMEM, VMEM, ANY, VMEM],
        VMEM,
        floats(width, front_count * size),
        scratch_shapes=[
            pltpu.VMEM((width, front_count * size), jnp.float32),
            pltpu.SemaphoreType.DMA(()),
        ],
    )(owners, gathered, own, mapped)
    return (x_leaf[None], x_sep[None])


def solution(mesh):
    placed = (
        P("leaf", None, "front"),
        P("leaf", None, "front"),
        P("leaf", "front", None, None),
        P("leaf", "front", None, None),
        P("leaf", "front", None),
        P("leaf", "front", None),
        P("leaf", "front", None, None),
        P("leaf", "front", None, None),
    )
    return jax.shard_map(
        per_device,
        mesh=mesh,
        in_specs=placed,
        out_specs=(P("leaf", None, "front"), P("leaf", None, "front")),
        check_vma=False,
    )
```

```python
import jax
import jax.numpy as jnp
from jax import lax
from jax.experimental import pallas as pl
from jax.experimental.pallas import tpu as pltpu
from jax.sharding import PartitionSpec as P

NT = (((1,), (1,)), ((), ()))
NN = (((1,), (0,)), ((), ()))


def dot(left, right, dims):
    return lax.dot_general(left, right, dims, preferred_element_type=jnp.float32)


def split(value):
    high = value.astype(jnp.bfloat16)
    low = (value - high.astype(jnp.float32)).astype(jnp.bfloat16)
    return high, low


def three_parts(parts, rows, size):
    return parts[:rows, :size] + (parts[rows:, :size] + parts[:rows, size:])


def product(left, right, dims):
    along = 0 if dims is NT else 1
    parts = dot(jnp.concatenate(split(left), axis=0), jnp.concatenate(split(right), axis=along), dims)
    return three_parts(parts, left.shape[0], right.shape[0])


def select(left, chosen, dims):
    rows = left.shape[0]
    both = dot(jnp.concatenate(split(left), axis=0), chosen, dims)
    return both[:rows] + both[rows:]


def chosen_rows(row_index, block_rows):
    separator_row = lax.broadcasted_iota(jnp.int32, (block_rows, block_rows), 0)
    return jnp.where(separator_row == row_index, 1.0, 0.0).astype(jnp.bfloat16)


def place_of(owner, own_class):
    y, z = owner >> EDGE_BITS, owner & (EDGE - 1)
    relative = jnp.bitwise_xor(((y & 1) << 1) | (z & 1), own_class)
    return relative, ((y >> 1) << (EDGE_BITS - 1)) | (z >> 1)


def leaf_forward(
    class_ref, owner_ref, rhs_ref, inv_ref, update_ref, rows_ref, y_ref, *rest
):
    *class_refs, dense_ref = rest
    step = pl.program_id(0)
    count, size, _ = inv_ref.shape
    members = class_refs[0].shape[0]

    @pl.when(step == 0)
    def _():
        dense_ref[...] = jnp.zeros_like(dense_ref)

    leaf_y = [product(rhs_ref[:, f * size : (f + 1) * size], inv_ref[f], NT) for f in range(count)]
    for f in range(count):
        y_ref[f] = leaf_y[f]
    updates = [product(leaf_y[f], update_ref[f], NT) for f in range(count)]
    placed = [select(updates[f], chosen_rows(rows_ref[f], size), NT) for f in range(count)]
    for f in range(count):
        relative, place = place_of(owner_ref[step * count + f], class_ref[0])
        dense_ref[relative * members + place] = placed[f]

    @pl.when(step == pl.num_programs(0) - 1)
    def _():
        for k, class_ref_k in enumerate(class_refs):
            class_ref_k[...] = dense_ref[k * members : (k + 1) * members]


def coupled_inverse(inv_ref, couple_ref, after_ref, out_ref):
    out_ref[0] = product(inv_ref[...], couple_ref[...], NN)


def leaf_prepare(y_ref, inv_ref, update_ref, rows_ref, own_ref, mapped_ref):
    count, size, _ = inv_ref.shape
    for f in range(count):
        inverse = inv_ref[f]
        own_ref[:, f * size : (f + 1) * size] = product(y_ref[f], inverse, NN)
        mapped = jnp.concatenate(split(product(update_ref[f], inverse, NN)), axis=1)
        placed = dot(chosen_rows(rows_ref[f], size), mapped, NN)
        mapped_ref[f] = jnp.concatenate(split(placed[:, :size] + placed[:, size:]), axis=1)


def reduce_right(received_ref, rhs_ref, inv_ref, out_ref):
    reduced = rhs_ref[...] - jnp.sum(received_ref[...], axis=0)
    solved = product(reduced, inv_ref[...], NT)
    for copy in range(out_ref.shape[0]):
        out_ref[copy] = solved


def chain(group_ref, right_ref, coupled_ref, inv_ref, x_ref, copies_ref, scratch):
    groups = right_ref.shape[0]
    own = group_ref[0]
    solved = [right_ref[0]]
    for group in range(1, groups):
        coupled = coupled_ref[jnp.bitwise_xor(own, group)]
        solved.append(right_ref[group] - product(solved[-1], coupled, NT))
    residue = solved[-1]
    scratch[groups - 1] = residue
    for group in range(groups - 1, 0, -1):
        coupled = coupled_ref[jnp.bitwise_xor(own, group)]
        residue = solved[group - 1] - product(residue, coupled, NN)
        scratch[group - 1] = residue
    x_sep = product(scratch[own], inv_ref[...], NN)
    x_ref[...] = x_sep
    for copy in range(copies_ref.shape[0]):
        copies_ref[copy] = x_sep


def leaf_backward(
    class_ref, owner_ref, x0_ref, x1_ref, x2_ref, x3_ref, own_hbm, mapped_ref, out_ref, x_ref, own_ref, arrived
):
    count, size, _ = mapped_ref.shape
    rows = out_ref.shape[0]
    members = x0_ref.shape[0]
    fetch = pltpu.make_async_copy(own_hbm, own_ref, arrived)
    fetch.start()
    for k, class_ref_k in enumerate((x0_ref, x1_ref, x2_ref, x3_ref)):
        x_ref[k * members : (k + 1) * members] = class_ref_k[...]
    for f in range(count):
        relative, place = place_of(owner_ref[f], class_ref[0])
        owned = jnp.concatenate(split(x_ref[relative * members + place]), axis=0)
        out_ref[:, f * size : (f + 1) * size] = three_parts(dot(owned, mapped_ref[f], NN), rows, size)
    fetch.wait()
    out_ref[...] = own_ref[...] - out_ref[...]


EDGE_BITS = 3
EDGE = 1 << EDGE_BITS
CLASSES = 4
FORWARD_STEP = 14
PREPARE_STEP = 7
VMEM = pl.BlockSpec(memory_space=pltpu.VMEM)
SMEM = pl.BlockSpec(memory_space=pltpu.SMEM)
ANY = pl.BlockSpec(memory_space=pl.ANY)
PARAMS = pltpu.CompilerParams(vmem_limit_bytes=32 << 20)


def floats(*shape):
    return jax.ShapeDtypeStruct(shape, jnp.float32)


def call(body, in_specs, out_specs, out_shape, **rest):
    return pl.pallas_call(
        body,
        in_specs=in_specs,
        out_specs=out_specs,
        out_shape=out_shape,
        compiler_params=PARAMS,
        name=body.__name__,
        **rest,
    )


def pair(index):
    return index ^ 1


def other_pair(index):
    return (index - 1 if index % 2 == 0 else index + 1) % EDGE


def exchange_classes(values):
    moves = (
        lambda y, z: (y, pair(z)),
        lambda y, z: (pair(y), z),
        lambda y, z: (other_pair(y), other_pair(z)),
    )
    result = [values[0]]
    for value, move in zip(values[1:], moves):
        pairs = []
        for source in range(EDGE * EDGE):
            y, z = move(source // EDGE, source % EDGE)
            pairs.append((source, y * EDGE + z))
        result.append(lax.ppermute(value, "front", pairs))
    return result


def exchange_members(value):
    half = range(EDGE // 2)
    groups = [
        [(2 * i + a) * EDGE + 2 * j + b for i in half for j in half] for a in range(2) for b in range(2)
    ]
    return lax.all_to_all(value, "front", 0, 0, tiled=True, axis_index_groups=groups)


def gather_by_bits(value, axis):
    count, bit = lax.axis_size(axis), 1
    while bit < count:
        pairs = [(source, source ^ bit) for source in range(count)]
        value = jnp.concatenate([value, lax.ppermute(value, axis, pairs)], axis=0)
        bit *= 2
    return value


def per_device(
    rhs_leaf, rhs_sep, leaf_inv, leaf_update, update_rows, update_owner, sep_inv, sep_couple
):
    front_count, size = leaf_inv.shape[1], leaf_inv.shape[3]
    width = rhs_leaf.shape[1]
    groups = lax.axis_size("leaf")
    fronts = lax.axis_size("front")

    def stay(value):
        return pltpu.with_memory_space_constraint(value, pltpu.HBM)

    right_leaf, inverse, coupling = stay(rhs_leaf[0]), stay(leaf_inv[0]), stay(leaf_update[0])
    rows = stay(update_rows.reshape(front_count, 1, size))
    owners = stay(update_owner.reshape(front_count))
    separator_inverse, separator_couple = sep_inv[0, 0], sep_couple[0, 0]

    def specs(step):
        matrices = pl.BlockSpec((step, size, size), lambda s: (s, 0, 0))
        lines = pl.BlockSpec((step, 1, size), lambda s: (s, 0, 0))
        vectors = pl.BlockSpec((step, width, size), lambda s: (s, 0, 0))
        columns = pl.BlockSpec((width, step * size), lambda s: (0, s))
        return matrices, lines, vectors, columns

    matrices, lines, vectors, columns = specs(FORWARD_STEP)
    members = fronts // CLASSES
    one_class = pl.BlockSpec((members, width, size), lambda s: (0, 0, 0))
    front = lax.axis_index("front")
    own_class = (((front >> (EDGE_BITS - 1)) & 2) | (front & 1)).reshape(1)
    leaf_y, *by_class = call(
        leaf_forward,
        [SMEM, SMEM, columns, matrices, matrices, lines],
        [vectors] + [one_class] * CLASSES,
        [floats(front_count, width, size)] + [floats(members, width, size)] * CLASSES,
        grid=(front_count // FORWARD_STEP,),
        scratch_shapes=[pltpu.VMEM((fronts, width, size), jnp.float32)],
    )(own_class, owners, right_leaf, inverse, coupling, rows)
    first, second, third, fourth = exchange_classes(by_class)
    received = exchange_members((first + second) + (third + fourth))

    coupled = call(coupled_inverse, [VMEM, VMEM, ANY], VMEM, floats(1, size, size))(
        separator_inverse, separator_couple, leaf_y
    )
    coupled = gather_by_bits(coupled, "leaf")
    matrices, lines, vectors, columns = specs(PREPARE_STEP)
    own, mapped = call(
        leaf_prepare,
        [vectors, matrices, matrices, lines],
        [columns, pl.BlockSpec((PREPARE_STEP, size, 2 * size), lambda s: (s, 0, 0))],
        [
            floats(width, front_count * size),
            jax.ShapeDtypeStruct((front_count, size, 2 * size), jnp.bfloat16),
        ],
        grid=(front_count // PREPARE_STEP,),
    )(leaf_y, inverse, coupling, rows)

    own = stay(own)
    right = call(reduce_right, [VMEM, VMEM, VMEM], VMEM, floats(groups, width, size))(
        received, rhs_sep[0], separator_inverse
    )
    right = lax.all_to_all(right, "leaf", 0, 0, tiled=True)
    x_sep, copies = call(
        chain,
        [SMEM, VMEM, VMEM, VMEM],
        [VMEM, VMEM],
        [floats(width, size), floats(members, width, size)],
        scratch_shapes=[pltpu.VMEM((groups, width, size), jnp.float32)],
    )(lax.axis_index("leaf").reshape(1), right, coupled, separator_inverse)
    gathered, own, mapped = lax.optimization_barrier((exchange_members(copies), own, mapped))
    gathered = exchange_classes([gathered] * CLASSES)
    x_leaf = call(
        leaf_backward,
        [SMEM, SMEM, VMEM, VMEM, VMEM, VMEM, ANY, VMEM],
        VMEM,
        floats(width, front_count * size),
        scratch_shapes=[
            pltpu.VMEM((fronts, width, size), jnp.float32),
            pltpu.VMEM((width, front_count * size), jnp.float32),
            pltpu.SemaphoreType.DMA(()),
        ],
    )(own_class, owners, *gathered, own, mapped)
    return (x_leaf[None], x_sep[None])


def solution(mesh):
    placed = (
        P("leaf", None, "front"),
        P("leaf", None, "front"),
        P("leaf", "front", None, None),
        P("leaf", "front", None, None),
        P("leaf", "front", None),
        P("leaf", "front", None),
        P("leaf", "front", None, None),
        P("leaf", "front", None, None),
    )
    return jax.shard_map(
        per_device,
        mesh=mesh,
        in_specs=placed,
        out_specs=(P("leaf", None, "front"), P("leaf", None, "front")),
        check_vma=False,
    )
```

```python
import jax
import jax.numpy as jnp
from jax import lax
from jax.experimental import pallas as pl
from jax.experimental.pallas import tpu as pltpu
from jax.sharding import PartitionSpec as P

NT = (((1,), (1,)), ((), ()))
NN = (((1,), (0,)), ((), ()))


def dot(left, right, dims):
    return lax.dot_general(left, right, dims, preferred_element_type=jnp.float32)


def split(value):
    high = value.astype(jnp.bfloat16)
    low = (value - high.astype(jnp.float32)).astype(jnp.bfloat16)
    return high, low


def three_parts(parts, rows, size):
    return parts[:rows, :size] + (parts[rows:, :size] + parts[:rows, size:])


def product(left, right, dims):
    along = 0 if dims is NT else 1
    parts = dot(jnp.concatenate(split(left), axis=0), jnp.concatenate(split(right), axis=along), dims)
    return three_parts(parts, left.shape[0], right.shape[0])


def select(left, chosen, dims):
    rows = left.shape[0]
    both = dot(jnp.concatenate(split(left), axis=0), chosen, dims)
    return both[:rows] + both[rows:]


def chosen_rows(row_index, block_rows):
    separator_row = lax.broadcasted_iota(jnp.int32, (block_rows, block_rows), 0)
    return jnp.where(separator_row == row_index, 1.0, 0.0).astype(jnp.bfloat16)


def slot_of(owner):
    y, z = owner >> EDGE_BITS, owner & (EDGE - 1)
    place = ((y >> 1) << (EDGE_BITS - 1)) | (z >> 1)
    return (((y & 1) << 1) | (z & 1)) * (EDGE * EDGE // CLASSES) + place


def leaf_forward(owner_ref, rhs_ref, inv_ref, update_ref, rows_ref, y_ref, dense_ref):
    step = pl.program_id(0)
    count, size, _ = inv_ref.shape

    @pl.when(step == 0)
    def _():
        dense_ref[...] = jnp.zeros_like(dense_ref)

    leaf_y = [product(rhs_ref[:, f * size : (f + 1) * size], inv_ref[f], NT) for f in range(count)]
    for f in range(count):
        y_ref[f] = leaf_y[f]
    updates = [product(leaf_y[f], update_ref[f], NT) for f in range(count)]
    placed = [select(updates[f], chosen_rows(rows_ref[f], size), NT) for f in range(count)]
    for f in range(count):
        dense_ref[slot_of(owner_ref[step * count + f])] = placed[f]


def coupled_inverse(inv_ref, couple_ref, after_ref, out_ref):
    out_ref[0] = product(inv_ref[...], couple_ref[...], NN)


def leaf_prepare(y_ref, inv_ref, update_ref, rows_ref, own_ref, mapped_ref):
    count, size, _ = inv_ref.shape
    for f in range(count):
        inverse = inv_ref[f]
        own_ref[:, f * size : (f + 1) * size] = product(y_ref[f], inverse, NN)
        mapped = jnp.concatenate(split(product(update_ref[f], inverse, NN)), axis=1)
        placed = dot(chosen_rows(rows_ref[f], size), mapped, NN)
        mapped_ref[f] = jnp.concatenate(split(placed[:, :size] + placed[:, size:]), axis=1)


def reduce_right(received_ref, rhs_ref, inv_ref, out_ref):
    reduced = rhs_ref[...] - jnp.sum(received_ref[...], axis=0)
    solved = product(reduced, inv_ref[...], NT)
    for copy in range(out_ref.shape[0]):
        out_ref[copy] = solved


def chain(group_ref, right_ref, coupled_ref, inv_ref, x_ref, copies_ref, scratch):
    groups = right_ref.shape[0]
    own = group_ref[0]
    solved = [right_ref[0]]
    for group in range(1, groups):
        coupled = coupled_ref[jnp.bitwise_xor(own, group)]
        solved.append(right_ref[group] - product(solved[-1], coupled, NT))
    residue = solved[-1]
    scratch[groups - 1] = residue
    for group in range(groups - 1, 0, -1):
        coupled = coupled_ref[jnp.bitwise_xor(own, group)]
        residue = solved[group - 1] - product(residue, coupled, NN)
        scratch[group - 1] = residue
    x_sep = product(scratch[own], inv_ref[...], NN)
    x_ref[...] = x_sep
    for copy in range(copies_ref.shape[0]):
        copies_ref[copy] = x_sep


def leaf_backward(owner_ref, x_ref, own_hbm, mapped_ref, out_hbm, own_ref, out_ref, own_arrived, stored):
    count, size, _ = mapped_ref.shape
    rows = out_ref.shape[0]
    fetch = pltpu.make_async_copy(own_hbm, own_ref, own_arrived)
    fetch.start()
    width = BACKWARD_CHUNK * size
    stores = []
    for first in range(0, count, BACKWARD_CHUNK):
        mapped = []
        for f in range(first, first + BACKWARD_CHUNK):
            owned = jnp.concatenate(split(x_ref[slot_of(owner_ref[f])]), axis=0)
            mapped.append(three_parts(dot(owned, mapped_ref[f], NN), rows, size))
        if first == 0:
            fetch.wait()
        for k, value in enumerate(mapped):
            here = slice((first + k) * size, (first + k + 1) * size)
            out_ref[:, here] = own_ref[:, here] - value
        here = slice(first * size, first * size + width)
        store = pltpu.make_async_copy(
            out_ref.at[:, here], out_hbm.at[:, here], stored.at[first // BACKWARD_CHUNK]
        )
        store.start()
        stores.append(store)
    for store in stores:
        store.wait()


EDGE_BITS = 3
EDGE = 1 << EDGE_BITS
CLASSES = 4
BACKWARD_CHUNK = 7
FORWARD_STEP = 14
PREPARE_STEP = 7
VMEM = pl.BlockSpec(memory_space=pltpu.VMEM)
SMEM = pl.BlockSpec(memory_space=pltpu.SMEM)
ANY = pl.BlockSpec(memory_space=pl.ANY)
PARAMS = pltpu.CompilerParams(vmem_limit_bytes=32 << 20)


def floats(*shape):
    return jax.ShapeDtypeStruct(shape, jnp.float32)


def call(body, in_specs, out_specs, out_shape, **rest):
    return pl.pallas_call(
        body,
        in_specs=in_specs,
        out_specs=out_specs,
        out_shape=out_shape,
        compiler_params=PARAMS,
        name=body.__name__,
        **rest,
    )


def exchange(value, groups_of_leaf):
    fronts = lax.axis_size("front")
    groups = [
        [leaf * fronts + front for front in group]
        for leaf in range(lax.axis_size("leaf"))
        for group in groups_of_leaf(leaf)
    ]
    return lax.all_to_all(value, ("leaf", "front"), 0, 0, tiled=True, axis_index_groups=groups)


def neighbours(leaf):
    groups = []
    for y in range(leaf % 2, EDGE + leaf % 2, 2):
        for z in range(leaf % 2, EDGE + leaf % 2, 2):
            four = [((y + a) % EDGE, (z + b) % EDGE) for a in range(2) for b in range(2)]
            four.sort(key=lambda at: (at[0] % 2, at[1] % 2))
            groups.append([a * EDGE + b for a, b in four])
    return groups


def members(leaf):
    half = range(EDGE // 2)
    return [[(2 * i + a) * EDGE + 2 * j + b for i in half for j in half] for a in range(2) for b in range(2)]


def gather_by_bits(value, axis):
    count, bit = lax.axis_size(axis), 1
    while bit < count:
        pairs = [(source, source ^ bit) for source in range(count)]
        value = jnp.concatenate([value, lax.ppermute(value, axis, pairs)], axis=0)
        bit *= 2
    return value


def per_device(
    rhs_leaf, rhs_sep, leaf_inv, leaf_update, update_rows, update_owner, sep_inv, sep_couple
):
    front_count, size = leaf_inv.shape[1], leaf_inv.shape[3]
    width = rhs_leaf.shape[1]
    groups = lax.axis_size("leaf")
    fronts = lax.axis_size("front")

    def stay(value):
        return pltpu.with_memory_space_constraint(value, pltpu.HBM)

    right_leaf, inverse, coupling = stay(rhs_leaf[0]), stay(leaf_inv[0]), stay(leaf_update[0])
    rows = stay(update_rows.reshape(front_count, 1, size))
    owners = stay(update_owner.reshape(front_count))
    separator_inverse, separator_couple = sep_inv[0, 0], sep_couple[0, 0]

    def specs(step):
        matrices = pl.BlockSpec((step, size, size), lambda s: (s, 0, 0))
        lines = pl.BlockSpec((step, 1, size), lambda s: (s, 0, 0))
        vectors = pl.BlockSpec((step, width, size), lambda s: (s, 0, 0))
        columns = pl.BlockSpec((width, step * size), lambda s: (0, s))
        return matrices, lines, vectors, columns

    matrices, lines, vectors, columns = specs(FORWARD_STEP)
    whole = pl.BlockSpec((fronts, width, size), lambda s: (0, 0, 0))
    leaf_y, dense = call(
        leaf_forward,
        [SMEM, columns, matrices, matrices, lines],
        [vectors, whole],
        [floats(front_count, width, size), floats(fronts, width, size)],
        grid=(front_count // FORWARD_STEP,),
    )(owners, right_leaf, inverse, coupling, rows)
    received = exchange(dense, neighbours).reshape(CLASSES, fronts // CLASSES, width, size)
    received = exchange(jnp.sum(received, axis=0), members)

    coupled = call(coupled_inverse, [VMEM, VMEM, ANY], VMEM, floats(1, size, size))(
        separator_inverse, separator_couple, leaf_y
    )
    coupled = gather_by_bits(coupled, "leaf")
    matrices, lines, vectors, columns = specs(PREPARE_STEP)
    own, mapped = call(
        leaf_prepare,
        [vectors, matrices, matrices, lines],
        [columns, pl.BlockSpec((PREPARE_STEP, size, 2 * size), lambda s: (s, 0, 0))],
        [
            floats(width, front_count * size),
            jax.ShapeDtypeStruct((front_count, size, 2 * size), jnp.bfloat16),
        ],
        grid=(front_count // PREPARE_STEP,),
    )(leaf_y, inverse, coupling, rows)

    own = stay(own)
    right = call(reduce_right, [VMEM, VMEM, VMEM], VMEM, floats(groups, width, size))(
        received, rhs_sep[0], separator_inverse
    )
    right = lax.all_to_all(right, "leaf", 0, 0, tiled=True)
    x_sep, copies = call(
        chain,
        [SMEM, VMEM, VMEM, VMEM],
        [VMEM, VMEM],
        [floats(width, size), floats(fronts // CLASSES, width, size)],
        scratch_shapes=[pltpu.VMEM((groups, width, size), jnp.float32)],
    )(lax.axis_index("leaf").reshape(1), right, coupled, separator_inverse)
    gathered, own, mapped = lax.optimization_barrier((exchange(copies, members), own, mapped))
    gathered = jnp.broadcast_to(gathered[None], (CLASSES, *gathered.shape)).reshape(fronts, width, size)
    gathered = exchange(gathered, neighbours)
    x_leaf = call(
        leaf_backward,
        [SMEM, VMEM, ANY, VMEM],
        ANY,
        floats(width, front_count * size),
        scratch_shapes=[
            pltpu.VMEM((width, front_count * size), jnp.float32),
            pltpu.VMEM((width, front_count * size), jnp.float32),
            pltpu.SemaphoreType.DMA(()),
            pltpu.SemaphoreType.DMA((front_count // BACKWARD_CHUNK,)),
        ],
    )(owners, gathered, own, mapped)
    return (x_leaf[None], x_sep[None])


def solution(mesh):
    placed = (
        P("leaf", None, "front"),
        P("leaf", None, "front"),
        P("leaf", "front", None, None),
        P("leaf", "front", None, None),
        P("leaf", "front", None),
        P("leaf", "front", None),
        P("leaf", "front", None, None),
        P("leaf", "front", None, None),
    )
    return jax.shard_map(
        per_device,
        mesh=mesh,
        in_specs=placed,
        out_specs=(P("leaf", None, "front"), P("leaf", None, "front")),
        check_vma=False,
    )
```

```python
import jax
import jax.numpy as jnp
from jax import lax
from jax.experimental import pallas as pl
from jax.experimental.pallas import tpu as pltpu
from jax.sharding import PartitionSpec as P

NT = (((1,), (1,)), ((), ()))
NN = (((1,), (0,)), ((), ()))


def dot(left, right, dims):
    return lax.dot_general(left, right, dims, preferred_element_type=jnp.float32)


def split(value):
    high = value.astype(jnp.bfloat16)
    low = (value - high.astype(jnp.float32)).astype(jnp.bfloat16)
    return high, low


def three_parts(parts, rows, size):
    return parts[:rows, :size] + (parts[rows:, :size] + parts[:rows, size:])


def product(left, right, dims):
    along = 0 if dims is NT else 1
    parts = dot(jnp.concatenate(split(left), axis=0), jnp.concatenate(split(right), axis=along), dims)
    return three_parts(parts, left.shape[0], right.shape[0])


def select(left, chosen, dims):
    rows = left.shape[0]
    both = dot(jnp.concatenate(split(left), axis=0), chosen, dims)
    return both[:rows] + both[rows:]


def chosen_rows(row_index, block_rows):
    separator_row = lax.broadcasted_iota(jnp.int32, (block_rows, block_rows), 0)
    return jnp.where(separator_row == row_index, 1.0, 0.0).astype(jnp.bfloat16)


def slot_of(owner):
    y, z = owner >> EDGE_BITS, owner & (EDGE - 1)
    place = ((y >> 1) << (EDGE_BITS - 1)) | (z >> 1)
    return (((y & 1) << 1) | (z & 1)) * (EDGE * EDGE // CLASSES) + place


def leaf_forward(owner_ref, rhs_ref, inv_ref, update_ref, rows_ref, y_ref, dense_ref):
    step = pl.program_id(0)
    count, size, _ = inv_ref.shape

    @pl.when(step == 0)
    def _():
        dense_ref[...] = jnp.zeros_like(dense_ref)

    leaf_y = [product(rhs_ref[:, f * size : (f + 1) * size], inv_ref[f], NT) for f in range(count)]
    for f in range(count):
        y_ref[f] = leaf_y[f]
    updates = [product(leaf_y[f], update_ref[f], NT) for f in range(count)]
    placed = [select(updates[f], chosen_rows(rows_ref[f], size), NT) for f in range(count)]
    for f in range(count):
        dense_ref[slot_of(owner_ref[step * count + f])] = placed[f]


def coupled_inverse(inv_ref, couple_ref, after_ref, out_ref):
    out_ref[0] = product(inv_ref[...], couple_ref[...], NN)


def leaf_prepare(y_ref, inv_ref, update_ref, rows_ref, mapped_ref):
    count, size, _ = inv_ref.shape
    for f in range(count):
        inverse = inv_ref[f]
        mapped_ref[f, size:] = jnp.concatenate(split(product(y_ref[f], inverse, NN)), axis=1)
        mapped = jnp.concatenate(split(product(update_ref[f], inverse, NN)), axis=1)
        placed = dot(chosen_rows(rows_ref[f], size), mapped, NN)
        mapped_ref[f, :size] = jnp.concatenate(split(placed[:, :size] + placed[:, size:]), axis=1)


def reduce_right(received_ref, rhs_ref, inv_ref, out_ref):
    reduced = rhs_ref[...] - jnp.sum(received_ref[...], axis=0)
    solved = product(reduced, inv_ref[...], NT)
    for copy in range(out_ref.shape[0]):
        out_ref[copy] = solved


def chain(group_ref, right_ref, coupled_ref, inv_ref, x_ref, copies_ref, scratch):
    groups = right_ref.shape[0]
    own = group_ref[0]
    solved = [right_ref[0]]
    for group in range(1, groups):
        coupled = coupled_ref[jnp.bitwise_xor(own, group)]
        solved.append(right_ref[group] - product(solved[-1], coupled, NT))
    residue = solved[-1]
    scratch[groups - 1] = residue
    for group in range(groups - 1, 0, -1):
        coupled = coupled_ref[jnp.bitwise_xor(own, group)]
        residue = solved[group - 1] - product(residue, coupled, NN)
        scratch[group - 1] = residue
    x_sep = product(scratch[own], inv_ref[...], NN)
    x_ref[...] = x_sep
    for copy in range(copies_ref.shape[0]):
        copies_ref[copy] = x_sep


def leaf_backward(owner_ref, x_ref, mapped_ref, out_hbm, out_ref, stored):
    count = mapped_ref.shape[0]
    rows = out_ref.shape[0]
    size = out_ref.shape[1] // count
    stores = []
    for f in range(count):
        owned = jnp.concatenate(split(x_ref[slot_of(owner_ref[f])]), axis=0)
        picked = three_parts(dot(owned, mapped_ref[f, :size], NN), rows, size)
        own = mapped_ref[f, size:].astype(jnp.float32)
        out_ref[:, f * size : (f + 1) * size] = (own[:, :size] + own[:, size:]) - picked
        if (f + 1) % BACKWARD_CHUNK == 0:
            here = slice((f + 1 - BACKWARD_CHUNK) * size, (f + 1) * size)
            store = pltpu.make_async_copy(
                out_ref.at[:, here], out_hbm.at[:, here], stored.at[f // BACKWARD_CHUNK]
            )
            store.start()
            stores.append(store)
    for store in stores:
        store.wait()


EDGE_BITS = 3
EDGE = 1 << EDGE_BITS
CLASSES = 4
BACKWARD_CHUNK = 7
FORWARD_STEP = 14
PREPARE_STEP = 7
VMEM = pl.BlockSpec(memory_space=pltpu.VMEM)
SMEM = pl.BlockSpec(memory_space=pltpu.SMEM)
ANY = pl.BlockSpec(memory_space=pl.ANY)
PARAMS = pltpu.CompilerParams(vmem_limit_bytes=32 << 20)


def floats(*shape):
    return jax.ShapeDtypeStruct(shape, jnp.float32)


def call(body, in_specs, out_specs, out_shape, **rest):
    return pl.pallas_call(
        body,
        in_specs=in_specs,
        out_specs=out_specs,
        out_shape=out_shape,
        compiler_params=PARAMS,
        name=body.__name__,
        **rest,
    )


def exchange(value, groups_of_leaf):
    fronts = lax.axis_size("front")
    groups = [
        [leaf * fronts + front for front in group]
        for leaf in range(lax.axis_size("leaf"))
        for group in groups_of_leaf(leaf)
    ]
    return lax.all_to_all(value, ("leaf", "front"), 0, 0, tiled=True, axis_index_groups=groups)


def neighbours(leaf):
    groups = []
    for y in range(leaf % 2, EDGE + leaf % 2, 2):
        for z in range(leaf % 2, EDGE + leaf % 2, 2):
            four = [((y + a) % EDGE, (z + b) % EDGE) for a in range(2) for b in range(2)]
            four.sort(key=lambda at: (at[0] % 2, at[1] % 2))
            groups.append([a * EDGE + b for a, b in four])
    return groups


def members(leaf):
    half = range(EDGE // 2)
    return [[(2 * i + a) * EDGE + 2 * j + b for i in half for j in half] for a in range(2) for b in range(2)]


def gather_by_bits(value, axis):
    count, bit = lax.axis_size(axis), 1
    while bit < count:
        pairs = [(source, source ^ bit) for source in range(count)]
        value = jnp.concatenate([value, lax.ppermute(value, axis, pairs)], axis=0)
        bit *= 2
    return value


def per_device(
    rhs_leaf, rhs_sep, leaf_inv, leaf_update, update_rows, update_owner, sep_inv, sep_couple
):
    front_count, size = leaf_inv.shape[1], leaf_inv.shape[3]
    width = rhs_leaf.shape[1]
    groups = lax.axis_size("leaf")
    fronts = lax.axis_size("front")

    def stay(value):
        return pltpu.with_memory_space_constraint(value, pltpu.HBM)

    right_leaf, inverse, coupling = stay(rhs_leaf[0]), stay(leaf_inv[0]), stay(leaf_update[0])
    rows = stay(update_rows.reshape(front_count, 1, size))
    owners = stay(update_owner.reshape(front_count))
    separator_inverse, separator_couple = sep_inv[0, 0], sep_couple[0, 0]

    def specs(step):
        matrices = pl.BlockSpec((step, size, size), lambda s: (s, 0, 0))
        lines = pl.BlockSpec((step, 1, size), lambda s: (s, 0, 0))
        vectors = pl.BlockSpec((step, width, size), lambda s: (s, 0, 0))
        columns = pl.BlockSpec((width, step * size), lambda s: (0, s))
        return matrices, lines, vectors, columns

    matrices, lines, vectors, columns = specs(FORWARD_STEP)
    whole = pl.BlockSpec((fronts, width, size), lambda s: (0, 0, 0))
    leaf_y, dense = call(
        leaf_forward,
        [SMEM, columns, matrices, matrices, lines],
        [vectors, whole],
        [floats(front_count, width, size), floats(fronts, width, size)],
        grid=(front_count // FORWARD_STEP,),
    )(owners, right_leaf, inverse, coupling, rows)
    received = exchange(dense, neighbours).reshape(CLASSES, fronts // CLASSES, width, size)
    received = exchange(jnp.sum(received, axis=0), members)

    coupled = call(coupled_inverse, [VMEM, VMEM, ANY], VMEM, floats(1, size, size))(
        separator_inverse, separator_couple, leaf_y
    )
    coupled = gather_by_bits(coupled, "leaf")
    matrices, lines, vectors, columns = specs(PREPARE_STEP)
    mapped = call(
        leaf_prepare,
        [vectors, matrices, matrices, lines],
        pl.BlockSpec((PREPARE_STEP, size + width, 2 * size), lambda s: (s, 0, 0)),
        jax.ShapeDtypeStruct((front_count, size + width, 2 * size), jnp.bfloat16),
        grid=(front_count // PREPARE_STEP,),
    )(leaf_y, inverse, coupling, rows)

    right = call(reduce_right, [VMEM, VMEM, VMEM], VMEM, floats(groups, width, size))(
        received, rhs_sep[0], separator_inverse
    )
    group = lax.axis_index("leaf").reshape(1)
    right, coupled, group, separator_inverse = lax.optimization_barrier(
        (right, coupled, group, separator_inverse)
    )
    right = lax.all_to_all(right, "leaf", 0, 0, tiled=True)
    x_sep, copies = call(
        chain,
        [SMEM, VMEM, VMEM, VMEM],
        [VMEM, VMEM],
        [floats(width, size), floats(fronts // CLASSES, width, size)],
        scratch_shapes=[pltpu.VMEM((groups, width, size), jnp.float32)],
    )(group, right, coupled, separator_inverse)
    gathered, mapped = lax.optimization_barrier((exchange(copies, members), mapped))
    gathered = jnp.broadcast_to(gathered[None], (CLASSES, *gathered.shape)).reshape(fronts, width, size)
    gathered = exchange(gathered, neighbours)
    x_leaf = call(
        leaf_backward,
        [SMEM, VMEM, VMEM],
        ANY,
        floats(width, front_count * size),
        scratch_shapes=[
            pltpu.VMEM((width, front_count * size), jnp.float32),
            pltpu.SemaphoreType.DMA((front_count // BACKWARD_CHUNK,)),
        ],
    )(update_owner.reshape(front_count), gathered, mapped)
    return (x_leaf[None], x_sep[None])


def solution(mesh):
    placed = (
        P("leaf", None, "front"),
        P("leaf", None, "front"),
        P("leaf", "front", None, None),
        P("leaf", "front", None, None),
        P("leaf", "front", None),
        P("leaf", "front", None),
        P("leaf", "front", None, None),
        P("leaf", "front", None, None),
    )
    return jax.shard_map(
        per_device,
        mesh=mesh,
        in_specs=placed,
        out_specs=(P("leaf", None, "front"), P("leaf", None, "front")),
        check_vma=False,
    )
```

```python
import jax
import jax.numpy as jnp
from jax import lax
from jax.experimental import pallas as pl
from jax.experimental.pallas import tpu as pltpu
from jax.sharding import PartitionSpec as P

NT = (((1,), (1,)), ((), ()))
NN = (((1,), (0,)), ((), ()))


def dot(left, right, dims):
    return lax.dot_general(left, right, dims, preferred_element_type=jnp.float32)


def split(value):
    high = value.astype(jnp.bfloat16)
    low = (value - high.astype(jnp.float32)).astype(jnp.bfloat16)
    return high, low


def three_parts(parts, rows, size):
    return parts[:rows, :size] + (parts[rows:, :size] + parts[:rows, size:])


def product(left, right, dims):
    along = 0 if dims is NT else 1
    parts = dot(jnp.concatenate(split(left), axis=0), jnp.concatenate(split(right), axis=along), dims)
    return three_parts(parts, left.shape[0], right.shape[0])


def select(left, chosen, dims):
    rows = left.shape[0]
    both = dot(jnp.concatenate(split(left), axis=0), chosen, dims)
    return both[:rows] + both[rows:]


def chosen_rows(row_index, block_rows):
    separator_row = lax.broadcasted_iota(jnp.int32, (block_rows, block_rows), 0)
    return jnp.where(separator_row == row_index, 1.0, 0.0).astype(jnp.bfloat16)


def slot_of(owner):
    y, z = owner >> EDGE_BITS, owner & (EDGE - 1)
    place = ((y >> 1) << (EDGE_BITS - 1)) | (z >> 1)
    return (((y & 1) << 1) | (z & 1)) * (EDGE * EDGE // CLASSES) + place


def leaf_forward(owner_ref, rhs_ref, inv_ref, update_ref, rows_ref, y_ref, dense_ref):
    step = pl.program_id(0)
    count, size, _ = inv_ref.shape

    @pl.when(step == 0)
    def _():
        dense_ref[...] = jnp.zeros_like(dense_ref)

    leaf_y = [product(rhs_ref[:, f * size : (f + 1) * size], inv_ref[f], NT) for f in range(count)]
    for f in range(count):
        y_ref[f] = leaf_y[f]
    updates = [product(leaf_y[f], update_ref[f], NT) for f in range(count)]
    placed = [select(updates[f], chosen_rows(rows_ref[f], size), NT) for f in range(count)]
    for f in range(count):
        dense_ref[slot_of(owner_ref[step * count + f])] = placed[f]


def coupled_inverse(inv_ref, couple_ref, after_ref, out_ref):
    out_ref[0] = product(inv_ref[...], couple_ref[...], NN)


def leaf_prepare(y_ref, inv_ref, update_ref, rows_ref, mapped_ref):
    count, size, _ = inv_ref.shape
    for f in range(count):
        inverse = inv_ref[f]
        mapped_ref[f, size:] = jnp.concatenate(split(product(y_ref[f], inverse, NN)), axis=1)
        mapped = jnp.concatenate(split(product(update_ref[f], inverse, NN)), axis=1)
        placed = dot(chosen_rows(rows_ref[f], size), mapped, NN)
        mapped_ref[f, :size] = jnp.concatenate(split(placed[:, :size] + placed[:, size:]), axis=1)


def reduce_right(received_ref, rhs_ref, inv_ref, out_ref):
    reduced = rhs_ref[...] - jnp.sum(received_ref[...], axis=0)
    solved = product(reduced, inv_ref[...], NT)
    for copy in range(out_ref.shape[0]):
        out_ref[copy] = solved


def chain(group_ref, right_ref, coupled_ref, inv_ref, x_ref, copies_ref, scratch):
    groups = right_ref.shape[0]
    own = group_ref[0]
    solved = [right_ref[0]]
    for group in range(1, groups):
        coupled = coupled_ref[jnp.bitwise_xor(own, group)]
        solved.append(right_ref[group] - product(solved[-1], coupled, NT))
    residue = solved[-1]
    scratch[groups - 1] = residue
    for group in range(groups - 1, 0, -1):
        coupled = coupled_ref[jnp.bitwise_xor(own, group)]
        residue = solved[group - 1] - product(residue, coupled, NN)
        scratch[group - 1] = residue
    x_sep = product(scratch[own], inv_ref[...], NN)
    x_ref[...] = x_sep
    for copy in range(copies_ref.shape[0]):
        copies_ref[copy] = x_sep


def leaf_backward(owner_ref, x_ref, early_ref, late_ref, out_hbm, out_ref, stored):
    half = early_ref.shape[0]
    count = half + late_ref.shape[0]
    rows = out_ref.shape[0]
    size = out_ref.shape[1] // count
    stores = []
    for f in range(count):
        owned = jnp.concatenate(split(x_ref[slot_of(owner_ref[f])]), axis=0)
        mapped_ref, at = (early_ref, f) if f < half else (late_ref, f - half)
        picked = three_parts(dot(owned, mapped_ref[at, :size], NN), rows, size)
        own = mapped_ref[at, size:].astype(jnp.float32)
        out_ref[:, f * size : (f + 1) * size] = (own[:, :size] + own[:, size:]) - picked
        if (f + 1) % BACKWARD_CHUNK == 0:
            here = slice((f + 1 - BACKWARD_CHUNK) * size, (f + 1) * size)
            store = pltpu.make_async_copy(
                out_ref.at[:, here], out_hbm.at[:, here], stored.at[f // BACKWARD_CHUNK]
            )
            store.start()
            stores.append(store)
    for store in stores:
        store.wait()


EDGE_BITS = 3
EDGE = 1 << EDGE_BITS
CLASSES = 4
BACKWARD_CHUNK = 7
FORWARD_STEP = 14
PREPARE_STEP = 7
VMEM = pl.BlockSpec(memory_space=pltpu.VMEM)
SMEM = pl.BlockSpec(memory_space=pltpu.SMEM)
ANY = pl.BlockSpec(memory_space=pl.ANY)
PARAMS = pltpu.CompilerParams(vmem_limit_bytes=32 << 20)


def floats(*shape):
    return jax.ShapeDtypeStruct(shape, jnp.float32)


def call(body, in_specs, out_specs, out_shape, **rest):
    return pl.pallas_call(
        body,
        in_specs=in_specs,
        out_specs=out_specs,
        out_shape=out_shape,
        compiler_params=PARAMS,
        name=body.__name__,
        **rest,
    )


def exchange(value, groups_of_leaf):
    fronts = lax.axis_size("front")
    groups = [
        [leaf * fronts + front for front in group]
        for leaf in range(lax.axis_size("leaf"))
        for group in groups_of_leaf(leaf)
    ]
    return lax.all_to_all(value, ("leaf", "front"), 0, 0, tiled=True, axis_index_groups=groups)


def neighbours(leaf):
    groups = []
    for y in range(leaf % 2, EDGE + leaf % 2, 2):
        for z in range(leaf % 2, EDGE + leaf % 2, 2):
            four = [((y + a) % EDGE, (z + b) % EDGE) for a in range(2) for b in range(2)]
            four.sort(key=lambda at: (at[0] % 2, at[1] % 2))
            groups.append([a * EDGE + b for a, b in four])
    return groups


def members(leaf):
    half = range(EDGE // 2)
    return [[(2 * i + a) * EDGE + 2 * j + b for i in half for j in half] for a in range(2) for b in range(2)]


def gather_by_bits(value, axis):
    count, bit = lax.axis_size(axis), 1
    while bit < count:
        pairs = [(source, source ^ bit) for source in range(count)]
        value = jnp.concatenate([value, lax.ppermute(value, axis, pairs)], axis=0)
        bit *= 2
    return value


def per_device(
    rhs_leaf, rhs_sep, leaf_inv, leaf_update, update_rows, update_owner, sep_inv, sep_couple
):
    front_count, size = leaf_inv.shape[1], leaf_inv.shape[3]
    width = rhs_leaf.shape[1]
    groups = lax.axis_size("leaf")
    fronts = lax.axis_size("front")

    def stay(value):
        return pltpu.with_memory_space_constraint(value, pltpu.HBM)

    right_leaf, inverse, coupling = stay(rhs_leaf[0]), stay(leaf_inv[0]), stay(leaf_update[0])
    rows = stay(update_rows.reshape(front_count, 1, size))
    owners = stay(update_owner.reshape(front_count))
    separator_inverse, separator_couple = sep_inv[0, 0], sep_couple[0, 0]

    def specs(step):
        matrices = pl.BlockSpec((step, size, size), lambda s: (s, 0, 0))
        lines = pl.BlockSpec((step, 1, size), lambda s: (s, 0, 0))
        vectors = pl.BlockSpec((step, width, size), lambda s: (s, 0, 0))
        columns = pl.BlockSpec((width, step * size), lambda s: (0, s))
        return matrices, lines, vectors, columns

    matrices, lines, vectors, columns = specs(FORWARD_STEP)
    whole = pl.BlockSpec((fronts, width, size), lambda s: (0, 0, 0))
    leaf_y, dense = call(
        leaf_forward,
        [SMEM, columns, matrices, matrices, lines],
        [vectors, whole],
        [floats(front_count, width, size), floats(fronts, width, size)],
        grid=(front_count // FORWARD_STEP,),
    )(owners, right_leaf, inverse, coupling, rows)
    received = exchange(dense, neighbours).reshape(CLASSES, fronts // CLASSES, width, size)
    received = exchange(jnp.sum(received, axis=0), members)

    coupled = call(coupled_inverse, [VMEM, VMEM, ANY], VMEM, floats(1, size, size))(
        separator_inverse, separator_couple, leaf_y
    )
    coupled = gather_by_bits(coupled, "leaf")
    steps = front_count // PREPARE_STEP // 2

    def prepare(start):
        def some(*block):
            return pl.BlockSpec((PREPARE_STEP, *block), lambda s: (s + start, 0, 0))

        return call(
            leaf_prepare,
            [some(width, size), some(size, size), some(size, size), some(1, size)],
            pl.BlockSpec((PREPARE_STEP, size + width, 2 * size), lambda s: (s, 0, 0)),
            jax.ShapeDtypeStruct((steps * PREPARE_STEP, size + width, 2 * size), jnp.bfloat16),
            grid=(steps,),
        )(leaf_y, inverse, coupling, rows)

    early, late = prepare(0), prepare(steps)

    right = call(reduce_right, [VMEM, VMEM, VMEM], VMEM, floats(groups, width, size))(
        received, rhs_sep[0], separator_inverse
    )
    right = lax.all_to_all(right, "leaf", 0, 0, tiled=True)
    x_sep, copies = call(
        chain,
        [SMEM, VMEM, VMEM, VMEM],
        [VMEM, VMEM],
        [floats(width, size), floats(fronts // CLASSES, width, size)],
        scratch_shapes=[pltpu.VMEM((groups, width, size), jnp.float32)],
    )(lax.axis_index("leaf").reshape(1), right, coupled, separator_inverse)
    gathered, early = lax.optimization_barrier((exchange(copies, members), early))
    gathered = jnp.broadcast_to(gathered[None], (CLASSES, *gathered.shape)).reshape(fronts, width, size)
    gathered = exchange(gathered, neighbours)
    x_leaf = call(
        leaf_backward,
        [SMEM, VMEM, VMEM, VMEM],
        ANY,
        floats(width, front_count * size),
        scratch_shapes=[
            pltpu.VMEM((width, front_count * size), jnp.float32),
            pltpu.SemaphoreType.DMA((front_count // BACKWARD_CHUNK,)),
        ],
    )(update_owner.reshape(front_count), gathered, early, late)
    return (x_leaf[None], x_sep[None])


def solution(mesh):
    placed = (
        P("leaf", None, "front"),
        P("leaf", None, "front"),
        P("leaf", "front", None, None),
        P("leaf", "front", None, None),
        P("leaf", "front", None),
        P("leaf", "front", None),
        P("leaf", "front", None, None),
        P("leaf", "front", None, None),
    )
    return jax.shard_map(
        per_device,
        mesh=mesh,
        in_specs=placed,
        out_specs=(P("leaf", None, "front"), P("leaf", None, "front")),
        check_vma=False,
    )
```

```python
import jax
import jax.numpy as jnp
from jax import lax
from jax.experimental import pallas as pl
from jax.experimental.pallas import tpu as pltpu
from jax.sharding import PartitionSpec as P

NT = (((1,), (1,)), ((), ()))
NN = (((1,), (0,)), ((), ()))


def dot(left, right, dims):
    return lax.dot_general(left, right, dims, preferred_element_type=jnp.float32)


def split(value):
    high = value.astype(jnp.bfloat16)
    low = (value - high.astype(jnp.float32)).astype(jnp.bfloat16)
    return high, low


def three_parts(parts, rows, size):
    return parts[:rows, :size] + (parts[rows:, :size] + parts[:rows, size:])


def product(left, right, dims):
    along = 0 if dims is NT else 1
    parts = dot(jnp.concatenate(split(left), axis=0), jnp.concatenate(split(right), axis=along), dims)
    return three_parts(parts, left.shape[0], right.shape[0])


def select(left, chosen, dims):
    rows = left.shape[0]
    both = dot(jnp.concatenate(split(left), axis=0), chosen, dims)
    return both[:rows] + both[rows:]


def chosen_rows(row_index, block_rows):
    separator_row = lax.broadcasted_iota(jnp.int32, (block_rows, block_rows), 0)
    return jnp.where(separator_row == row_index, 1.0, 0.0).astype(jnp.bfloat16)


def slot_of(owner):
    y, z = owner >> EDGE_BITS, owner & (EDGE - 1)
    place = ((y >> 1) << (EDGE_BITS - 1)) | (z >> 1)
    return (((y & 1) << 1) | (z & 1)) * (EDGE * EDGE // CLASSES) + place


def leaf_forward(owner_ref, rhs_ref, inv_ref, update_ref, rows_ref, y_ref, dense_ref):
    step = pl.program_id(0)
    count, size, _ = inv_ref.shape

    @pl.when(step == 0)
    def _():
        dense_ref[...] = jnp.zeros_like(dense_ref)

    leaf_y = [product(rhs_ref[:, f * size : (f + 1) * size], inv_ref[f], NT) for f in range(count)]
    for f in range(count):
        y_ref[f] = leaf_y[f]
    updates = [product(leaf_y[f], update_ref[f], NT) for f in range(count)]
    placed = [select(updates[f], chosen_rows(rows_ref[f], size), NT) for f in range(count)]
    for f in range(count):
        dense_ref[slot_of(owner_ref[step * count + f])] = placed[f]


def coupled_inverse(inv_ref, couple_ref, after_ref, out_ref):
    out_ref[0] = product(inv_ref[...], couple_ref[...], NN)


def leaf_prepare(y_ref, inv_ref, update_ref, rows_ref, mapped_ref):
    count, size, _ = inv_ref.shape
    for f in range(count):
        inverse = inv_ref[f]
        mapped_ref[f, size:] = jnp.concatenate(split(product(y_ref[f], inverse, NN)), axis=1)
        mapped = jnp.concatenate(split(product(update_ref[f], inverse, NN)), axis=1)
        placed = dot(chosen_rows(rows_ref[f], size), mapped, NN)
        mapped_ref[f, :size] = jnp.concatenate(split(placed[:, :size] + placed[:, size:]), axis=1)


def reduce_right(received_ref, rhs_ref, inv_ref, out_ref):
    reduced = rhs_ref[...] - jnp.sum(received_ref[...], axis=0)
    solved = product(reduced, inv_ref[...], NT)
    for copy in range(out_ref.shape[0]):
        out_ref[copy] = solved


def chain(group_ref, right_ref, coupled_ref, inv_ref, x_ref, copies_ref, scratch):
    groups = right_ref.shape[0]
    own = group_ref[0]
    solved = [right_ref[0]]
    for group in range(1, groups):
        coupled = coupled_ref[jnp.bitwise_xor(own, group)]
        solved.append(right_ref[group] - product(solved[-1], coupled, NT))
    residue = solved[-1]
    scratch[groups - 1] = residue
    for group in range(groups - 1, 0, -1):
        coupled = coupled_ref[jnp.bitwise_xor(own, group)]
        residue = solved[group - 1] - product(residue, coupled, NN)
        scratch[group - 1] = residue
    x_sep = product(scratch[own], inv_ref[...], NN)
    x_ref[...] = x_sep
    for copy in range(copies_ref.shape[0]):
        copies_ref[copy] = x_sep


def leaf_backward(owner_ref, x_ref, mapped_ref, out_hbm, out_ref, stored):
    count = mapped_ref.shape[0]
    rows = out_ref.shape[0]
    size = out_ref.shape[1] // count
    stores = []
    for f in range(count):
        owned = jnp.concatenate(split(x_ref[slot_of(owner_ref[f])]), axis=0)
        picked = three_parts(dot(owned, mapped_ref[f, :size], NN), rows, size)
        own = mapped_ref[f, size:].astype(jnp.float32)
        out_ref[:, f * size : (f + 1) * size] = (own[:, :size] + own[:, size:]) - picked
        if (f + 1) % BACKWARD_CHUNK == 0:
            here = slice((f + 1 - BACKWARD_CHUNK) * size, (f + 1) * size)
            store = pltpu.make_async_copy(
                out_ref.at[:, here], out_hbm.at[:, here], stored.at[f // BACKWARD_CHUNK]
            )
            store.start()
            stores.append(store)
    for store in stores:
        store.wait()


EDGE_BITS = 3
EDGE = 1 << EDGE_BITS
CLASSES = 4
BACKWARD_CHUNK = 7
FORWARD_STEP = 14
PREPARE_STEP = 7
VMEM = pl.BlockSpec(memory_space=pltpu.VMEM)
SMEM = pl.BlockSpec(memory_space=pltpu.SMEM)
ANY = pl.BlockSpec(memory_space=pl.ANY)
PARAMS = pltpu.CompilerParams(vmem_limit_bytes=32 << 20)


def floats(*shape):
    return jax.ShapeDtypeStruct(shape, jnp.float32)


def call(body, in_specs, out_specs, out_shape, **rest):
    return pl.pallas_call(
        body,
        in_specs=in_specs,
        out_specs=out_specs,
        out_shape=out_shape,
        compiler_params=PARAMS,
        name=body.__name__,
        **rest,
    )


def exchange(value, groups_of_leaf):
    fronts = lax.axis_size("front")
    groups = [
        [leaf * fronts + front for front in group]
        for leaf in range(lax.axis_size("leaf"))
        for group in groups_of_leaf(leaf)
    ]
    return lax.all_to_all(value, ("leaf", "front"), 0, 0, tiled=True, axis_index_groups=groups)


def neighbours(leaf):
    groups = []
    for y in range(leaf % 2, EDGE + leaf % 2, 2):
        for z in range(leaf % 2, EDGE + leaf % 2, 2):
            four = [((y + a) % EDGE, (z + b) % EDGE) for a in range(2) for b in range(2)]
            four.sort(key=lambda at: (at[0] % 2, at[1] % 2))
            groups.append([a * EDGE + b for a, b in four])
    return groups


def members(leaf):
    half = range(EDGE // 2)
    return [[(2 * i + a) * EDGE + 2 * j + b for i in half for j in half] for a in range(2) for b in range(2)]


def gather_by_bits(value, axis):
    count, bit = lax.axis_size(axis), 1
    while bit < count:
        pairs = [(source, source ^ bit) for source in range(count)]
        value = jnp.concatenate([value, lax.ppermute(value, axis, pairs)], axis=0)
        bit *= 2
    return value


def per_device(
    rhs_leaf, rhs_sep, leaf_inv, leaf_update, update_rows, update_owner, sep_inv, sep_couple
):
    front_count, size = leaf_inv.shape[1], leaf_inv.shape[3]
    width = rhs_leaf.shape[1]
    groups = lax.axis_size("leaf")
    fronts = lax.axis_size("front")

    def stay(value):
        return pltpu.with_memory_space_constraint(value, pltpu.HBM)

    right_leaf, inverse, coupling = stay(rhs_leaf[0]), stay(leaf_inv[0]), stay(leaf_update[0])
    rows = stay(update_rows.reshape(front_count, 1, size))
    owners = stay(update_owner.reshape(front_count))
    separator_inverse, separator_couple = sep_inv[0, 0], sep_couple[0, 0]

    def specs(step):
        matrices = pl.BlockSpec((step, size, size), lambda s: (s, 0, 0))
        lines = pl.BlockSpec((step, 1, size), lambda s: (s, 0, 0))
        vectors = pl.BlockSpec((step, width, size), lambda s: (s, 0, 0))
        columns = pl.BlockSpec((width, step * size), lambda s: (0, s))
        return matrices, lines, vectors, columns

    matrices, lines, vectors, columns = specs(FORWARD_STEP)
    whole = pl.BlockSpec((fronts, width, size), lambda s: (0, 0, 0))
    leaf_y, dense = call(
        leaf_forward,
        [SMEM, columns, matrices, matrices, lines],
        [vectors, whole],
        [floats(front_count, width, size), floats(fronts, width, size)],
        grid=(front_count // FORWARD_STEP,),
    )(owners, right_leaf, inverse, coupling, rows)
    received = exchange(dense, neighbours).reshape(CLASSES, fronts // CLASSES, width, size)
    received = exchange(jnp.sum(received, axis=0), members)

    coupled = call(coupled_inverse, [VMEM, VMEM, ANY], VMEM, floats(1, size, size))(
        separator_inverse, separator_couple, leaf_y
    )
    coupled = gather_by_bits(coupled, "leaf")
    matrices, lines, vectors, columns = specs(PREPARE_STEP)
    mapped = call(
        leaf_prepare,
        [vectors, matrices, matrices, lines],
        pl.BlockSpec((PREPARE_STEP, size + width, 2 * size), lambda s: (s, 0, 0)),
        jax.ShapeDtypeStruct((front_count, size + width, 2 * size), jnp.bfloat16),
        grid=(front_count // PREPARE_STEP,),
    )(leaf_y, inverse, coupling, rows)

    right = call(reduce_right, [VMEM, VMEM, VMEM], VMEM, floats(groups, width, size))(
        received, rhs_sep[0], separator_inverse
    )
    right = lax.all_to_all(right, "leaf", 0, 0, tiled=True)
    x_sep, copies = call(
        chain,
        [SMEM, VMEM, VMEM, VMEM],
        [VMEM, VMEM],
        [floats(width, size), floats(fronts // CLASSES, width, size)],
        scratch_shapes=[pltpu.VMEM((groups, width, size), jnp.float32)],
    )(lax.axis_index("leaf").reshape(1), right, coupled, separator_inverse)
    gathered, mapped = lax.optimization_barrier((exchange(copies, members), mapped))
    gathered = jnp.broadcast_to(gathered[None], (CLASSES, *gathered.shape)).reshape(fronts, width, size)
    gathered = exchange(gathered, neighbours)
    x_leaf = call(
        leaf_backward,
        [SMEM, VMEM, VMEM],
        ANY,
        floats(width, front_count * size),
        scratch_shapes=[
            pltpu.VMEM((width, front_count * size), jnp.float32),
            pltpu.SemaphoreType.DMA((front_count // BACKWARD_CHUNK,)),
        ],
    )(update_owner.reshape(front_count), gathered, mapped)
    return (x_leaf[None], x_sep[None])


def solution(mesh):
    placed = (
        P("leaf", None, "front"),
        P("leaf", None, "front"),
        P("leaf", "front", None, None),
        P("leaf", "front", None, None),
        P("leaf", "front", None),
        P("leaf", "front", None),
        P("leaf", "front", None, None),
        P("leaf", "front", None, None),
    )
    return jax.shard_map(
        per_device,
        mesh=mesh,
        in_specs=placed,
        out_specs=(P("leaf", None, "front"), P("leaf", None, "front")),
        check_vma=False,
    )
```

```python
import jax
import jax.numpy as jnp
from jax import lax
from jax.experimental import pallas as pl
from jax.experimental.pallas import tpu as pltpu
from jax.sharding import PartitionSpec as P

NT = (((1,), (1,)), ((), ()))
NN = (((1,), (0,)), ((), ()))


def dot(left, right, dims):
    return lax.dot_general(left, right, dims, preferred_element_type=jnp.float32)


def split(value):
    high = value.astype(jnp.bfloat16)
    low = (value - high.astype(jnp.float32)).astype(jnp.bfloat16)
    return high, low


def three_parts(parts, rows, size):
    return parts[:rows, :size] + (parts[rows:, :size] + parts[:rows, size:])


def product(left, right, dims):
    along = 0 if dims is NT else 1
    parts = dot(jnp.concatenate(split(left), axis=0), jnp.concatenate(split(right), axis=along), dims)
    return three_parts(parts, left.shape[0], right.shape[0])


def select(left, chosen, dims):
    rows = left.shape[0]
    both = dot(jnp.concatenate(split(left), axis=0), chosen, dims)
    return both[:rows] + both[rows:]


def chosen_rows(row_index, block_rows):
    separator_row = lax.broadcasted_iota(jnp.int32, (block_rows, block_rows), 0)
    return jnp.where(separator_row == row_index, 1.0, 0.0).astype(jnp.bfloat16)


def slot_of(owner):
    y, z = owner >> EDGE_BITS, owner & (EDGE - 1)
    place = ((y >> 1) << (EDGE_BITS - 1)) | (z >> 1)
    return (((y & 1) << 1) | (z & 1)) * (EDGE * EDGE // CLASSES) + place


def leaf_forward(owner_ref, rhs_ref, inv_ref, update_ref, rows_ref, y_ref, dense_ref):
    step = pl.program_id(0)
    count, size, _ = inv_ref.shape

    @pl.when(step == 0)
    def _():
        dense_ref[...] = jnp.zeros_like(dense_ref)

    leaf_y = [product(rhs_ref[:, f * size : (f + 1) * size], inv_ref[f], NT) for f in range(count)]
    for f in range(count):
        y_ref[f] = leaf_y[f]
    updates = [product(leaf_y[f], update_ref[f], NT) for f in range(count)]
    placed = [select(updates[f], chosen_rows(rows_ref[f], size), NT) for f in range(count)]
    for f in range(count):
        dense_ref[slot_of(owner_ref[step * count + f])] = placed[f]


def coupled_inverse(inv_ref, couple_ref, after_ref, out_ref):
    out_ref[0] = product(inv_ref[...], couple_ref[...], NN)


def leaf_prepare(y_ref, inv_ref, update_ref, rows_ref, mapped_ref):
    count, size, _ = inv_ref.shape
    fronts = range(count)
    both = [product(jnp.concatenate([update_ref[f], y_ref[f]], axis=0), inv_ref[f], NN) for f in fronts]
    mapped = [jnp.concatenate(split(both[f][:size]), axis=1) for f in fronts]
    for f in fronts:
        mapped_ref[f, size:] = jnp.concatenate(split(both[f][size:]), axis=1)
    placed = [dot(chosen_rows(rows_ref[f], size), mapped[f], NN) for f in fronts]
    for f in fronts:
        whole = placed[f][:, :size] + placed[f][:, size:]
        mapped_ref[f, :size] = jnp.concatenate(split(whole), axis=1)


def reduce_right(received_ref, rhs_ref, inv_ref, out_ref):
    reduced = rhs_ref[...] - jnp.sum(received_ref[...], axis=0)
    solved = product(reduced, inv_ref[...], NT)
    for copy in range(out_ref.shape[0]):
        out_ref[copy] = solved


def chain(group_ref, right_ref, coupled_ref, inv_ref, x_ref, copies_ref, scratch):
    groups = right_ref.shape[0]
    own = group_ref[0]
    solved = [right_ref[0]]
    for group in range(1, groups):
        coupled = coupled_ref[jnp.bitwise_xor(own, group)]
        solved.append(right_ref[group] - product(solved[-1], coupled, NT))
    residue = solved[-1]
    scratch[groups - 1] = residue
    for group in range(groups - 1, 0, -1):
        coupled = coupled_ref[jnp.bitwise_xor(own, group)]
        residue = solved[group - 1] - product(residue, coupled, NN)
        scratch[group - 1] = residue
    x_sep = product(scratch[own], inv_ref[...], NN)
    x_ref[...] = x_sep
    for copy in range(copies_ref.shape[0]):
        copies_ref[copy] = x_sep


def leaf_backward(owner_ref, x_ref, mapped_ref, out_hbm, out_ref, stored):
    count = mapped_ref.shape[0]
    rows = out_ref.shape[0]
    size = out_ref.shape[1] // count
    stores = []
    for f in range(count):
        owned = jnp.concatenate(split(x_ref[slot_of(owner_ref[f])]), axis=0)
        picked = three_parts(dot(owned, mapped_ref[f, :size], NN), rows, size)
        own = mapped_ref[f, size:].astype(jnp.float32)
        out_ref[:, f * size : (f + 1) * size] = (own[:, :size] + own[:, size:]) - picked
        if (f + 1) % BACKWARD_CHUNK == 0:
            here = slice((f + 1 - BACKWARD_CHUNK) * size, (f + 1) * size)
            store = pltpu.make_async_copy(
                out_ref.at[:, here], out_hbm.at[:, here], stored.at[f // BACKWARD_CHUNK]
            )
            store.start()
            stores.append(store)
    for store in stores:
        store.wait()


EDGE_BITS = 3
EDGE = 1 << EDGE_BITS
CLASSES = 4
BACKWARD_CHUNK = 7
FORWARD_STEP = 14
PREPARE_STEP = 14
VMEM = pl.BlockSpec(memory_space=pltpu.VMEM)
SMEM = pl.BlockSpec(memory_space=pltpu.SMEM)
ANY = pl.BlockSpec(memory_space=pl.ANY)
PARAMS = pltpu.CompilerParams(vmem_limit_bytes=32 << 20)


def floats(*shape):
    return jax.ShapeDtypeStruct(shape, jnp.float32)


def call(body, in_specs, out_specs, out_shape, **rest):
    return pl.pallas_call(
        body,
        in_specs=in_specs,
        out_specs=out_specs,
        out_shape=out_shape,
        compiler_params=PARAMS,
        name=body.__name__,
        **rest,
    )


def exchange(value, groups_of_leaf):
    fronts = lax.axis_size("front")
    groups = [
        [leaf * fronts + front for front in group]
        for leaf in range(lax.axis_size("leaf"))
        for group in groups_of_leaf(leaf)
    ]
    return lax.all_to_all(value, ("leaf", "front"), 0, 0, tiled=True, axis_index_groups=groups)


def neighbours(leaf):
    groups = []
    for y in range(leaf % 2, EDGE + leaf % 2, 2):
        for z in range(leaf % 2, EDGE + leaf % 2, 2):
            four = [((y + a) % EDGE, (z + b) % EDGE) for a in range(2) for b in range(2)]
            four.sort(key=lambda at: (at[0] % 2, at[1] % 2))
            groups.append([a * EDGE + b for a, b in four])
    return groups


def members(leaf):
    half = range(EDGE // 2)
    return [[(2 * i + a) * EDGE + 2 * j + b for i in half for j in half] for a in range(2) for b in range(2)]


def gather_by_bits(value, axis):
    count, bit = lax.axis_size(axis), 1
    while bit < count:
        pairs = [(source, source ^ bit) for source in range(count)]
        value = jnp.concatenate([value, lax.ppermute(value, axis, pairs)], axis=0)
        bit *= 2
    return value


def per_device(
    rhs_leaf, rhs_sep, leaf_inv, leaf_update, update_rows, update_owner, sep_inv, sep_couple
):
    front_count, size = leaf_inv.shape[1], leaf_inv.shape[3]
    width = rhs_leaf.shape[1]
    groups = lax.axis_size("leaf")
    fronts = lax.axis_size("front")

    def stay(value):
        return pltpu.with_memory_space_constraint(value, pltpu.HBM)

    right_leaf, inverse, coupling = stay(rhs_leaf[0]), stay(leaf_inv[0]), stay(leaf_update[0])
    rows = stay(update_rows.reshape(front_count, 1, size))
    owners = stay(update_owner.reshape(front_count))
    separator_inverse, separator_couple = sep_inv[0, 0], sep_couple[0, 0]

    def specs(step):
        matrices = pl.BlockSpec((step, size, size), lambda s: (s, 0, 0))
        lines = pl.BlockSpec((step, 1, size), lambda s: (s, 0, 0))
        vectors = pl.BlockSpec((step, width, size), lambda s: (s, 0, 0))
        columns = pl.BlockSpec((width, step * size), lambda s: (0, s))
        return matrices, lines, vectors, columns

    matrices, lines, vectors, columns = specs(FORWARD_STEP)
    whole = pl.BlockSpec((fronts, width, size), lambda s: (0, 0, 0))
    leaf_y, dense = call(
        leaf_forward,
        [SMEM, columns, matrices, matrices, lines],
        [vectors, whole],
        [floats(front_count, width, size), floats(fronts, width, size)],
        grid=(front_count // FORWARD_STEP,),
    )(owners, right_leaf, inverse, coupling, rows)
    received = exchange(dense, neighbours).reshape(CLASSES, fronts // CLASSES, width, size)
    received = exchange(jnp.sum(received, axis=0), members)

    coupled = call(coupled_inverse, [VMEM, VMEM, ANY], VMEM, floats(1, size, size))(
        separator_inverse, separator_couple, leaf_y
    )
    coupled = gather_by_bits(coupled, "leaf")
    matrices, lines, vectors, columns = specs(PREPARE_STEP)
    mapped = call(
        leaf_prepare,
        [vectors, matrices, matrices, lines],
        pl.BlockSpec((PREPARE_STEP, size + width, 2 * size), lambda s: (s, 0, 0)),
        jax.ShapeDtypeStruct((front_count, size + width, 2 * size), jnp.bfloat16),
        grid=(front_count // PREPARE_STEP,),
    )(leaf_y, inverse, coupling, rows)

    right = call(reduce_right, [VMEM, VMEM, VMEM], VMEM, floats(groups, width, size))(
        received, rhs_sep[0], separator_inverse
    )
    right = lax.all_to_all(right, "leaf", 0, 0, tiled=True)
    x_sep, copies = call(
        chain,
        [SMEM, VMEM, VMEM, VMEM],
        [VMEM, VMEM],
        [floats(width, size), floats(fronts // CLASSES, width, size)],
        scratch_shapes=[pltpu.VMEM((groups, width, size), jnp.float32)],
    )(lax.axis_index("leaf").reshape(1), right, coupled, separator_inverse)
    gathered, mapped = lax.optimization_barrier((exchange(copies, members), mapped))
    gathered = jnp.broadcast_to(gathered[None], (CLASSES, *gathered.shape)).reshape(fronts, width, size)
    gathered = exchange(gathered, neighbours)
    x_leaf = call(
        leaf_backward,
        [SMEM, VMEM, VMEM],
        ANY,
        floats(width, front_count * size),
        scratch_shapes=[
            pltpu.VMEM((width, front_count * size), jnp.float32),
            pltpu.SemaphoreType.DMA((front_count // BACKWARD_CHUNK,)),
        ],
    )(update_owner.reshape(front_count), gathered, mapped)
    return (x_leaf[None], x_sep[None])


def solution(mesh):
    placed = (
        P("leaf", None, "front"),
        P("leaf", None, "front"),
        P("leaf", "front", None, None),
        P("leaf", "front", None, None),
        P("leaf", "front", None),
        P("leaf", "front", None),
        P("leaf", "front", None, None),
        P("leaf", "front", None, None),
    )
    return jax.shard_map(
        per_device,
        mesh=mesh,
        in_specs=placed,
        out_specs=(P("leaf", None, "front"), P("leaf", None, "front")),
        check_vma=False,
    )
```

```python
import jax
import jax.numpy as jnp
from jax import lax
from jax.experimental import pallas as pl
from jax.experimental.pallas import tpu as pltpu
from jax.sharding import PartitionSpec as P

NT = (((1,), (1,)), ((), ()))
NN = (((1,), (0,)), ((), ()))


def dot(left, right, dims):
    return lax.dot_general(left, right, dims, preferred_element_type=jnp.float32)


def split(value):
    high = value.astype(jnp.bfloat16)
    low = (value - high.astype(jnp.float32)).astype(jnp.bfloat16)
    return high, low


def three_parts(parts, rows, size):
    return parts[:rows, :size] + (parts[rows:, :size] + parts[:rows, size:])


def product(left, right, dims):
    along = 0 if dims is NT else 1
    parts = dot(jnp.concatenate(split(left), axis=0), jnp.concatenate(split(right), axis=along), dims)
    return three_parts(parts, left.shape[0], right.shape[0])


def select(left, chosen, dims):
    rows = left.shape[0]
    both = dot(jnp.concatenate(split(left), axis=0), chosen, dims)
    return both[:rows] + both[rows:]


def chosen_rows(row_index, block_rows):
    separator_row = lax.broadcasted_iota(jnp.int32, (block_rows, block_rows), 0)
    return jnp.where(separator_row == row_index, 1.0, 0.0).astype(jnp.bfloat16)


def slot_of(owner):
    y, z = owner >> EDGE_BITS, owner & (EDGE - 1)
    place = ((y >> 1) << (EDGE_BITS - 1)) | (z >> 1)
    return (((y & 1) << 1) | (z & 1)) * (EDGE * EDGE // CLASSES) + place


def leaf_forward(owner_ref, rhs_ref, inv_ref, update_ref, rows_ref, y_ref, dense_ref):
    step = pl.program_id(0)
    count, size, _ = inv_ref.shape

    @pl.when(step == 0)
    def _():
        dense_ref[...] = jnp.zeros_like(dense_ref)

    leaf_y = [product(rhs_ref[:, f * size : (f + 1) * size], inv_ref[f], NT) for f in range(count)]
    for f in range(count):
        y_ref[f] = leaf_y[f]
    updates = [product(leaf_y[f], update_ref[f], NT) for f in range(count)]
    placed = [select(updates[f], chosen_rows(rows_ref[f], size), NT) for f in range(count)]
    for f in range(count):
        dense_ref[slot_of(owner_ref[step * count + f])] = placed[f]


def coupled_inverse(inv_ref, couple_ref, after_ref, out_ref):
    out_ref[0] = product(inv_ref[...], couple_ref[...], NN)


def leaf_prepare(y_ref, inv_ref, update_ref, rows_ref, mapped_ref):
    count, size, _ = inv_ref.shape
    fronts = range(count)
    both = [product(jnp.concatenate([update_ref[f], y_ref[f]], axis=0), inv_ref[f], NN) for f in fronts]
    mapped = [jnp.concatenate(split(both[f][:size]), axis=1) for f in fronts]
    for f in fronts:
        mapped_ref[f, size:] = jnp.concatenate(split(both[f][size:]), axis=1)
    placed = [dot(chosen_rows(rows_ref[f], size), mapped[f], NN) for f in fronts]
    for f in fronts:
        whole = placed[f][:, :size] + placed[f][:, size:]
        mapped_ref[f, :size] = jnp.concatenate(split(whole), axis=1)


def reduce_right(received_ref, rhs_ref, inv_ref, out_ref):
    reduced = rhs_ref[...] - jnp.sum(received_ref[...], axis=0)
    solved = product(reduced, inv_ref[...], NT)
    for copy in range(out_ref.shape[0]):
        out_ref[copy] = solved


def chain(group_ref, right_ref, coupled_ref, inv_ref, x_ref, copies_ref, scratch):
    groups = right_ref.shape[0]
    own = group_ref[0]
    solved = [right_ref[0]]
    for group in range(1, groups):
        coupled = coupled_ref[jnp.bitwise_xor(own, group)]
        solved.append(right_ref[group] - product(solved[-1], coupled, NT))
    residue = solved[-1]
    scratch[groups - 1] = residue
    for group in range(groups - 1, 0, -1):
        coupled = coupled_ref[jnp.bitwise_xor(own, group)]
        residue = solved[group - 1] - product(residue, coupled, NN)
        scratch[group - 1] = residue
    x_sep = product(scratch[own], inv_ref[...], NN)
    x_ref[...] = x_sep
    for copy in range(copies_ref.shape[0]):
        copies_ref[copy] = x_sep


def leaf_backward(owner_ref, x_ref, mapped_ref, out_hbm, out_ref, stored):
    count = mapped_ref.shape[0]
    rows = out_ref.shape[0]
    size = out_ref.shape[1] // count
    stores = []
    for f in range(count):
        owned = jnp.concatenate(split(x_ref[slot_of(owner_ref[f])]), axis=0)
        picked = three_parts(dot(owned, mapped_ref[f, :size], NN), rows, size)
        own = mapped_ref[f, size:].astype(jnp.float32)
        out_ref[:, f * size : (f + 1) * size] = (own[:, :size] + own[:, size:]) - picked
        if (f + 1) % BACKWARD_CHUNK == 0:
            here = slice((f + 1 - BACKWARD_CHUNK) * size, (f + 1) * size)
            store = pltpu.make_async_copy(
                out_ref.at[:, here], out_hbm.at[:, here], stored.at[f // BACKWARD_CHUNK]
            )
            store.start()
            stores.append(store)
    for store in stores:
        store.wait()


EDGE_BITS = 3
EDGE = 1 << EDGE_BITS
CLASSES = 4
BACKWARD_CHUNK = 7
FORWARD_STEP = 14
PREPARE_STEP = 14
VMEM = pl.BlockSpec(memory_space=pltpu.VMEM)
SMEM = pl.BlockSpec(memory_space=pltpu.SMEM)
ANY = pl.BlockSpec(memory_space=pl.ANY)
PARAMS = pltpu.CompilerParams(vmem_limit_bytes=32 << 20)


def floats(*shape):
    return jax.ShapeDtypeStruct(shape, jnp.float32)


def call(body, in_specs, out_specs, out_shape, **rest):
    return pl.pallas_call(
        body,
        in_specs=in_specs,
        out_specs=out_specs,
        out_shape=out_shape,
        compiler_params=PARAMS,
        name=body.__name__,
        **rest,
    )


def exchange(value, groups_of_leaf):
    fronts = lax.axis_size("front")
    groups = [
        [leaf * fronts + front for front in group]
        for leaf in range(lax.axis_size("leaf"))
        for group in groups_of_leaf(leaf)
    ]
    return lax.all_to_all(value, ("leaf", "front"), 0, 0, tiled=True, axis_index_groups=groups)


def neighbours(leaf):
    groups = []
    for y in range(leaf % 2, EDGE + leaf % 2, 2):
        for z in range(leaf % 2, EDGE + leaf % 2, 2):
            four = [((y + a) % EDGE, (z + b) % EDGE) for a in range(2) for b in range(2)]
            four.sort(key=lambda at: (at[0] % 2, at[1] % 2))
            groups.append([a * EDGE + b for a, b in four])
    return groups


def members(leaf):
    half = range(EDGE // 2)
    return [[(2 * i + a) * EDGE + 2 * j + b for i in half for j in half] for a in range(2) for b in range(2)]


def gather_by_bits(value, axis):
    count, bit = lax.axis_size(axis), 1
    while bit < count:
        pairs = [(source, source ^ bit) for source in range(count)]
        value = jnp.concatenate([value, lax.ppermute(value, axis, pairs)], axis=0)
        bit *= 2
    return value


def per_device(
    rhs_leaf, rhs_sep, leaf_inv, leaf_update, update_rows, update_owner, sep_inv, sep_couple
):
    front_count, size = leaf_inv.shape[1], leaf_inv.shape[3]
    width = rhs_leaf.shape[1]
    groups = lax.axis_size("leaf")
    fronts = lax.axis_size("front")

    def stay(value):
        return pltpu.with_memory_space_constraint(value, pltpu.HBM)

    right_leaf, inverse, coupling = stay(rhs_leaf[0]), stay(leaf_inv[0]), stay(leaf_update[0])
    rows = stay(update_rows.reshape(front_count, 1, size))
    owners = stay(update_owner.reshape(front_count))
    separator_inverse, separator_couple = sep_inv[0, 0], sep_couple[0, 0]

    def specs(step):
        matrices = pl.BlockSpec((step, size, size), lambda s: (s, 0, 0))
        lines = pl.BlockSpec((step, 1, size), lambda s: (s, 0, 0))
        vectors = pl.BlockSpec((step, width, size), lambda s: (s, 0, 0))
        columns = pl.BlockSpec((width, step * size), lambda s: (0, s))
        return matrices, lines, vectors, columns

    matrices, lines, vectors, columns = specs(FORWARD_STEP)
    whole = pl.BlockSpec((fronts, width, size), lambda s: (0, 0, 0))
    leaf_y, dense = call(
        leaf_forward,
        [SMEM, columns, matrices, matrices, lines],
        [vectors, whole],
        [floats(front_count, width, size), floats(fronts, width, size)],
        grid=(front_count // FORWARD_STEP,),
    )(owners, right_leaf, inverse, coupling, rows)
    received = exchange(dense, neighbours).reshape(CLASSES, fronts // CLASSES, width, size)
    received = exchange(jnp.sum(received, axis=0), members)

    coupled = call(coupled_inverse, [VMEM, VMEM, ANY], VMEM, floats(1, size, size))(
        separator_inverse, separator_couple, leaf_y
    )
    coupled = gather_by_bits(coupled, "leaf")
    matrices, lines, vectors, columns = specs(PREPARE_STEP)
    mapped = call(
        leaf_prepare,
        [vectors, matrices, matrices, lines],
        pl.BlockSpec((PREPARE_STEP, size + width, 2 * size), lambda s: (s, 0, 0)),
        jax.ShapeDtypeStruct((front_count, size + width, 2 * size), jnp.bfloat16),
        grid=(front_count // PREPARE_STEP,),
    )(leaf_y, inverse, coupling, rows)

    right = call(reduce_right, [VMEM, VMEM, VMEM], VMEM, floats(groups, width, size))(
        received, rhs_sep[0], separator_inverse
    )
    right, mapped = lax.optimization_barrier((lax.all_to_all(right, "leaf", 0, 0, tiled=True), mapped))
    x_sep, copies = call(
        chain,
        [SMEM, VMEM, VMEM, VMEM],
        [VMEM, VMEM],
        [floats(width, size), floats(fronts // CLASSES, width, size)],
        scratch_shapes=[pltpu.VMEM((groups, width, size), jnp.float32)],
    )(lax.axis_index("leaf").reshape(1), right, coupled, separator_inverse)
    gathered = exchange(copies, members)
    gathered = jnp.broadcast_to(gathered[None], (CLASSES, *gathered.shape)).reshape(fronts, width, size)
    gathered = exchange(gathered, neighbours)
    x_leaf = call(
        leaf_backward,
        [SMEM, VMEM, VMEM],
        ANY,
        floats(width, front_count * size),
        scratch_shapes=[
            pltpu.VMEM((width, front_count * size), jnp.float32),
            pltpu.SemaphoreType.DMA((front_count // BACKWARD_CHUNK,)),
        ],
    )(update_owner.reshape(front_count), gathered, mapped)
    return (x_leaf[None], x_sep[None])


def solution(mesh):
    placed = (
        P("leaf", None, "front"),
        P("leaf", None, "front"),
        P("leaf", "front", None, None),
        P("leaf", "front", None, None),
        P("leaf", "front", None),
        P("leaf", "front", None),
        P("leaf", "front", None, None),
        P("leaf", "front", None, None),
    )
    return jax.shard_map(
        per_device,
        mesh=mesh,
        in_specs=placed,
        out_specs=(P("leaf", None, "front"), P("leaf", None, "front")),
        check_vma=False,
    )
```

```python
import jax
import jax.numpy as jnp
from jax import lax
from jax.experimental import pallas as pl
from jax.experimental.pallas import tpu as pltpu
from jax.sharding import PartitionSpec as P

NT = (((1,), (1,)), ((), ()))
NN = (((1,), (0,)), ((), ()))


def dot(left, right, dims):
    return lax.dot_general(left, right, dims, preferred_element_type=jnp.float32)


def split(value):
    high = value.astype(jnp.bfloat16)
    low = (value - high.astype(jnp.float32)).astype(jnp.bfloat16)
    return high, low


def three_parts(parts, rows, size):
    return parts[:rows, :size] + (parts[rows:, :size] + parts[:rows, size:])


def product(left, right, dims):
    along = 0 if dims is NT else 1
    parts = dot(jnp.concatenate(split(left), axis=0), jnp.concatenate(split(right), axis=along), dims)
    return three_parts(parts, left.shape[0], right.shape[0])


def select(left, chosen, dims):
    rows = left.shape[0]
    both = dot(jnp.concatenate(split(left), axis=0), chosen, dims)
    return both[:rows] + both[rows:]


def chosen_rows(row_index, block_rows):
    separator_row = lax.broadcasted_iota(jnp.int32, (block_rows, block_rows), 0)
    return jnp.where(separator_row == row_index, 1.0, 0.0).astype(jnp.bfloat16)


def class_of(index):
    return (index & 1) ^ (index >> (EDGE_BITS - 1))


def slot_of(owner, leaf):
    y = ((owner >> EDGE_BITS) - (leaf & 1)) & (EDGE - 1)
    z = (owner - (leaf & 1)) & (EDGE - 1)
    place = ((y >> 1) << (EDGE_BITS - 1)) | (z >> 1)
    return ((class_of(y) << 1) | class_of(z)) * (EDGE * EDGE // CLASSES) + place


def leaf_forward(leaf_ref, owner_ref, rhs_ref, inv_ref, update_ref, rows_ref, y_ref, dense_ref):
    step = pl.program_id(0)
    count, size, _ = inv_ref.shape

    @pl.when(step == 0)
    def _():
        dense_ref[...] = jnp.zeros_like(dense_ref)

    leaf_y = [product(rhs_ref[:, f * size : (f + 1) * size], inv_ref[f], NT) for f in range(count)]
    for f in range(count):
        y_ref[f] = leaf_y[f]
    updates = [product(leaf_y[f], update_ref[f], NT) for f in range(count)]
    placed = [select(updates[f], chosen_rows(rows_ref[f], size), NT) for f in range(count)]
    for f in range(count):
        dense_ref[slot_of(owner_ref[step * count + f], leaf_ref[0])] = placed[f]


def coupled_inverse(inv_ref, couple_ref, after_ref, out_ref):
    out_ref[0] = product(inv_ref[...], couple_ref[...], NN)


def leaf_prepare(y_ref, inv_ref, update_ref, rows_ref, mapped_ref):
    count, size, _ = inv_ref.shape
    fronts = range(count)
    both = [product(jnp.concatenate([update_ref[f], y_ref[f]], axis=0), inv_ref[f], NN) for f in fronts]
    mapped = [jnp.concatenate(split(both[f][:size]), axis=1) for f in fronts]
    for f in fronts:
        mapped_ref[f, size:] = jnp.concatenate(split(both[f][size:]), axis=1)
    placed = [dot(chosen_rows(rows_ref[f], size), mapped[f], NN) for f in fronts]
    for f in fronts:
        whole = placed[f][:, :size] + placed[f][:, size:]
        mapped_ref[f, :size] = jnp.concatenate(split(whole), axis=1)


def reduce_right(received_ref, rhs_ref, inv_ref, out_ref):
    reduced = rhs_ref[...] - jnp.sum(received_ref[...], axis=0)
    solved = product(reduced, inv_ref[...], NT)
    for copy in range(out_ref.shape[0]):
        out_ref[copy] = solved


def chain(group_ref, right_ref, coupled_ref, inv_ref, x_ref, copies_ref, scratch):
    groups = right_ref.shape[0]
    own = group_ref[0]
    solved = [right_ref[0]]
    for group in range(1, groups):
        coupled = coupled_ref[jnp.bitwise_xor(own, group)]
        solved.append(right_ref[group] - product(solved[-1], coupled, NT))
    residue = solved[-1]
    scratch[groups - 1] = residue
    for group in range(groups - 1, 0, -1):
        coupled = coupled_ref[jnp.bitwise_xor(own, group)]
        residue = solved[group - 1] - product(residue, coupled, NN)
        scratch[group - 1] = residue
    x_sep = product(scratch[own], inv_ref[...], NN)
    x_ref[...] = x_sep
    for copy in range(copies_ref.shape[0]):
        copies_ref[copy] = x_sep


def leaf_backward(leaf_ref, owner_ref, x_ref, mapped_ref, out_hbm, out_ref, stored):
    count = mapped_ref.shape[0]
    rows = out_ref.shape[0]
    size = out_ref.shape[1] // count
    stores = []
    for f in range(count):
        owned = jnp.concatenate(split(x_ref[slot_of(owner_ref[f], leaf_ref[0])]), axis=0)
        picked = three_parts(dot(owned, mapped_ref[f, :size], NN), rows, size)
        own = mapped_ref[f, size:].astype(jnp.float32)
        out_ref[:, f * size : (f + 1) * size] = (own[:, :size] + own[:, size:]) - picked
        if (f + 1) % BACKWARD_CHUNK == 0:
            here = slice((f + 1 - BACKWARD_CHUNK) * size, (f + 1) * size)
            store = pltpu.make_async_copy(
                out_ref.at[:, here], out_hbm.at[:, here], stored.at[f // BACKWARD_CHUNK]
            )
            store.start()
            stores.append(store)
    for store in stores:
        store.wait()


EDGE_BITS = 3
EDGE = 1 << EDGE_BITS
CLASSES = 4
BACKWARD_CHUNK = 7
FORWARD_STEP = 14
PREPARE_STEP = 14
VMEM = pl.BlockSpec(memory_space=pltpu.VMEM)
SMEM = pl.BlockSpec(memory_space=pltpu.SMEM)
ANY = pl.BlockSpec(memory_space=pl.ANY)
PARAMS = pltpu.CompilerParams(vmem_limit_bytes=32 << 20)


def floats(*shape):
    return jax.ShapeDtypeStruct(shape, jnp.float32)


def call(body, in_specs, out_specs, out_shape, **rest):
    return pl.pallas_call(
        body,
        in_specs=in_specs,
        out_specs=out_specs,
        out_shape=out_shape,
        compiler_params=PARAMS,
        name=body.__name__,
        **rest,
    )


def exchange(value, groups_of_leaf):
    fronts = lax.axis_size("front")
    groups = [
        [leaf * fronts + front for front in group]
        for leaf in range(lax.axis_size("leaf"))
        for group in groups_of_leaf(leaf)
    ]
    return lax.all_to_all(value, ("leaf", "front"), 0, 0, tiled=True, axis_index_groups=groups)


def device(y, z, leaf):
    return (y + leaf % 2) % EDGE * EDGE + (z + leaf % 2) % EDGE


def of_class(first, kind):
    return first if class_of(first) == kind else first + 1


def neighbours(leaf):
    kinds = [(a, b) for a in range(2) for b in range(2)]
    pairs = range(0, EDGE, 2)
    return [[device(of_class(y, a), of_class(z, b), leaf) for a, b in kinds] for y in pairs for z in pairs]


def members(leaf):
    kinds = [(a, b) for a in range(2) for b in range(2)]
    pairs = range(0, EDGE, 2)
    return [[device(of_class(y, a), of_class(z, b), leaf) for y in pairs for z in pairs] for a, b in kinds]


def gather_by_bits(value, axis):
    count, bit = lax.axis_size(axis), 1
    while bit < count:
        pairs = [(source, source ^ bit) for source in range(count)]
        value = jnp.concatenate([value, lax.ppermute(value, axis, pairs)], axis=0)
        bit *= 2
    return value


def per_device(
    rhs_leaf, rhs_sep, leaf_inv, leaf_update, update_rows, update_owner, sep_inv, sep_couple
):
    front_count, size = leaf_inv.shape[1], leaf_inv.shape[3]
    width = rhs_leaf.shape[1]
    groups = lax.axis_size("leaf")
    fronts = lax.axis_size("front")

    def stay(value):
        return pltpu.with_memory_space_constraint(value, pltpu.HBM)

    right_leaf, inverse, coupling = stay(rhs_leaf[0]), stay(leaf_inv[0]), stay(leaf_update[0])
    rows = stay(update_rows.reshape(front_count, 1, size))
    owners = stay(update_owner.reshape(front_count))
    separator_inverse, separator_couple = sep_inv[0, 0], sep_couple[0, 0]

    def specs(step):
        matrices = pl.BlockSpec((step, size, size), lambda s: (s, 0, 0))
        lines = pl.BlockSpec((step, 1, size), lambda s: (s, 0, 0))
        vectors = pl.BlockSpec((step, width, size), lambda s: (s, 0, 0))
        columns = pl.BlockSpec((width, step * size), lambda s: (0, s))
        return matrices, lines, vectors, columns

    leaf = lax.axis_index("leaf").reshape(1)
    matrices, lines, vectors, columns = specs(FORWARD_STEP)
    whole = pl.BlockSpec((fronts, width, size), lambda s: (0, 0, 0))
    leaf_y, dense = call(
        leaf_forward,
        [SMEM, SMEM, columns, matrices, matrices, lines],
        [vectors, whole],
        [floats(front_count, width, size), floats(fronts, width, size)],
        grid=(front_count // FORWARD_STEP,),
    )(leaf, owners, right_leaf, inverse, coupling, rows)
    received = exchange(dense, neighbours).reshape(CLASSES, fronts // CLASSES, width, size)
    received = exchange(jnp.sum(received, axis=0), members)

    coupled = call(coupled_inverse, [VMEM, VMEM, ANY], VMEM, floats(1, size, size))(
        separator_inverse, separator_couple, leaf_y
    )
    coupled = gather_by_bits(coupled, "leaf")
    matrices, lines, vectors, columns = specs(PREPARE_STEP)
    mapped = call(
        leaf_prepare,
        [vectors, matrices, matrices, lines],
        pl.BlockSpec((PREPARE_STEP, size + width, 2 * size), lambda s: (s, 0, 0)),
        jax.ShapeDtypeStruct((front_count, size + width, 2 * size), jnp.bfloat16),
        grid=(front_count // PREPARE_STEP,),
    )(leaf_y, inverse, coupling, rows)

    right = call(reduce_right, [VMEM, VMEM, VMEM], VMEM, floats(groups, width, size))(
        received, rhs_sep[0], separator_inverse
    )
    right = lax.all_to_all(right, "leaf", 0, 0, tiled=True)
    x_sep, copies = call(
        chain,
        [SMEM, VMEM, VMEM, VMEM],
        [VMEM, VMEM],
        [floats(width, size), floats(fronts // CLASSES, width, size)],
        scratch_shapes=[pltpu.VMEM((groups, width, size), jnp.float32)],
    )(lax.axis_index("leaf").reshape(1), right, coupled, separator_inverse)
    gathered, mapped = lax.optimization_barrier((exchange(copies, members), mapped))
    gathered = jnp.broadcast_to(gathered[None], (CLASSES, *gathered.shape)).reshape(fronts, width, size)
    gathered = exchange(gathered, neighbours)
    x_leaf = call(
        leaf_backward,
        [SMEM, SMEM, VMEM, VMEM],
        ANY,
        floats(width, front_count * size),
        scratch_shapes=[
            pltpu.VMEM((width, front_count * size), jnp.float32),
            pltpu.SemaphoreType.DMA((front_count // BACKWARD_CHUNK,)),
        ],
    )(leaf, update_owner.reshape(front_count), gathered, mapped)
    return (x_leaf[None], x_sep[None])


def solution(mesh):
    placed = (
        P("leaf", None, "front"),
        P("leaf", None, "front"),
        P("leaf", "front", None, None),
        P("leaf", "front", None, None),
        P("leaf", "front", None),
        P("leaf", "front", None),
        P("leaf", "front", None, None),
        P("leaf", "front", None, None),
    )
    return jax.shard_map(
        per_device,
        mesh=mesh,
        in_specs=placed,
        out_specs=(P("leaf", None, "front"), P("leaf", None, "front")),
        check_vma=False,
    )
```

```python
import jax
import jax.numpy as jnp
from jax import lax
from jax.experimental import pallas as pl
from jax.experimental.pallas import tpu as pltpu
from jax.sharding import PartitionSpec as P

NT = (((1,), (1,)), ((), ()))
NN = (((1,), (0,)), ((), ()))


def dot(left, right, dims):
    return lax.dot_general(left, right, dims, preferred_element_type=jnp.float32)


def split(value):
    high = value.astype(jnp.bfloat16)
    low = (value - high.astype(jnp.float32)).astype(jnp.bfloat16)
    return high, low


def three_parts(parts, rows, size):
    return parts[:rows, :size] + (parts[rows:, :size] + parts[:rows, size:])


def product(left, right, dims):
    along = 0 if dims is NT else 1
    parts = dot(jnp.concatenate(split(left), axis=0), jnp.concatenate(split(right), axis=along), dims)
    return three_parts(parts, left.shape[0], right.shape[0])


def select(left, chosen, dims):
    rows = left.shape[0]
    both = dot(jnp.concatenate(split(left), axis=0), chosen, dims)
    return both[:rows] + both[rows:]


def chosen_rows(row_index, block_rows):
    separator_row = lax.broadcasted_iota(jnp.int32, (block_rows, block_rows), 0)
    return jnp.where(separator_row == row_index, 1.0, 0.0).astype(jnp.bfloat16)


def class_of(index):
    return (index & 1) ^ (index >> (EDGE_BITS - 1))


def slot_of(owner, leaf):
    shift = 1 - (leaf & 1)
    y = ((owner >> EDGE_BITS) - shift) & (EDGE - 1)
    z = (owner - shift) & (EDGE - 1)
    place = ((y >> 1) << (EDGE_BITS - 1)) | (z >> 1)
    return ((class_of(y) << 1) | class_of(z)) * (EDGE * EDGE // CLASSES) + place


def leaf_forward(leaf_ref, owner_ref, rhs_ref, inv_ref, update_ref, rows_ref, y_ref, dense_ref):
    step = pl.program_id(0)
    count, size, _ = inv_ref.shape

    @pl.when(step == 0)
    def _():
        dense_ref[...] = jnp.zeros_like(dense_ref)

    leaf_y = [product(rhs_ref[:, f * size : (f + 1) * size], inv_ref[f], NT) for f in range(count)]
    for f in range(count):
        y_ref[f] = leaf_y[f]
    updates = [product(leaf_y[f], update_ref[f], NT) for f in range(count)]
    placed = [select(updates[f], chosen_rows(rows_ref[f], size), NT) for f in range(count)]
    for f in range(count):
        dense_ref[slot_of(owner_ref[step * count + f], leaf_ref[0])] = placed[f]


def coupled_inverse(inv_ref, couple_ref, after_ref, out_ref):
    out_ref[0] = product(inv_ref[...], couple_ref[...], NN)


def leaf_prepare(y_ref, inv_ref, update_ref, rows_ref, mapped_ref):
    count, size, _ = inv_ref.shape
    fronts = range(count)
    both = [product(jnp.concatenate([update_ref[f], y_ref[f]], axis=0), inv_ref[f], NN) for f in fronts]
    mapped = [jnp.concatenate(split(both[f][:size]), axis=1) for f in fronts]
    for f in fronts:
        mapped_ref[f, size:] = jnp.concatenate(split(both[f][size:]), axis=1)
    placed = [dot(chosen_rows(rows_ref[f], size), mapped[f], NN) for f in fronts]
    for f in fronts:
        whole = placed[f][:, :size] + placed[f][:, size:]
        mapped_ref[f, :size] = jnp.concatenate(split(whole), axis=1)


def reduce_right(received_ref, rhs_ref, inv_ref, out_ref):
    reduced = rhs_ref[...] - jnp.sum(received_ref[...], axis=0)
    solved = product(reduced, inv_ref[...], NT)
    for copy in range(out_ref.shape[0]):
        out_ref[copy] = solved


def chain(group_ref, right_ref, coupled_ref, inv_ref, x_ref, copies_ref, scratch):
    groups = right_ref.shape[0]
    own = group_ref[0]
    solved = [right_ref[0]]
    for group in range(1, groups):
        coupled = coupled_ref[jnp.bitwise_xor(own, group)]
        solved.append(right_ref[group] - product(solved[-1], coupled, NT))
    residue = solved[-1]
    scratch[groups - 1] = residue
    for group in range(groups - 1, 0, -1):
        coupled = coupled_ref[jnp.bitwise_xor(own, group)]
        residue = solved[group - 1] - product(residue, coupled, NN)
        scratch[group - 1] = residue
    x_sep = product(scratch[own], inv_ref[...], NN)
    x_ref[...] = x_sep
    for copy in range(copies_ref.shape[0]):
        copies_ref[copy] = x_sep


def leaf_backward(leaf_ref, owner_ref, x_ref, mapped_ref, out_hbm, out_ref, stored):
    count = mapped_ref.shape[0]
    rows = out_ref.shape[0]
    size = out_ref.shape[1] // count
    stores = []
    for f in range(count):
        owned = jnp.concatenate(split(x_ref[slot_of(owner_ref[f], leaf_ref[0])]), axis=0)
        picked = three_parts(dot(owned, mapped_ref[f, :size], NN), rows, size)
        own = mapped_ref[f, size:].astype(jnp.float32)
        out_ref[:, f * size : (f + 1) * size] = (own[:, :size] + own[:, size:]) - picked
        if (f + 1) % BACKWARD_CHUNK == 0:
            here = slice((f + 1 - BACKWARD_CHUNK) * size, (f + 1) * size)
            store = pltpu.make_async_copy(
                out_ref.at[:, here], out_hbm.at[:, here], stored.at[f // BACKWARD_CHUNK]
            )
            store.start()
            stores.append(store)
    for store in stores:
        store.wait()


EDGE_BITS = 3
EDGE = 1 << EDGE_BITS
CLASSES = 4
BACKWARD_CHUNK = 7
FORWARD_STEP = 14
PREPARE_STEP = 14
VMEM = pl.BlockSpec(memory_space=pltpu.VMEM)
SMEM = pl.BlockSpec(memory_space=pltpu.SMEM)
ANY = pl.BlockSpec(memory_space=pl.ANY)
PARAMS = pltpu.CompilerParams(vmem_limit_bytes=32 << 20)


def floats(*shape):
    return jax.ShapeDtypeStruct(shape, jnp.float32)


def call(body, in_specs, out_specs, out_shape, **rest):
    return pl.pallas_call(
        body,
        in_specs=in_specs,
        out_specs=out_specs,
        out_shape=out_shape,
        compiler_params=PARAMS,
        name=body.__name__,
        **rest,
    )


def exchange(value, groups_of_leaf):
    fronts = lax.axis_size("front")
    groups = [
        [leaf * fronts + front for front in group]
        for leaf in range(lax.axis_size("leaf"))
        for group in groups_of_leaf(leaf)
    ]
    return lax.all_to_all(value, ("leaf", "front"), 0, 0, tiled=True, axis_index_groups=groups)


def device(y, z, leaf):
    shift = 1 - leaf % 2
    return (y + shift) % EDGE * EDGE + (z + shift) % EDGE


def of_class(first, kind):
    return first if class_of(first) == kind else first + 1


def neighbours(leaf):
    kinds = [(a, b) for a in range(2) for b in range(2)]
    pairs = range(0, EDGE, 2)
    return [[device(of_class(y, a), of_class(z, b), leaf) for a, b in kinds] for y in pairs for z in pairs]


def members(leaf):
    kinds = [(a, b) for a in range(2) for b in range(2)]
    pairs = range(0, EDGE, 2)
    return [[device(of_class(y, a), of_class(z, b), leaf) for y in pairs for z in pairs] for a, b in kinds]


def gather_by_bits(value, axis):
    count, bit = lax.axis_size(axis), 1
    while bit < count:
        pairs = [(source, source ^ bit) for source in range(count)]
        value = jnp.concatenate([value, lax.ppermute(value, axis, pairs)], axis=0)
        bit *= 2
    return value


def per_device(
    rhs_leaf, rhs_sep, leaf_inv, leaf_update, update_rows, update_owner, sep_inv, sep_couple
):
    front_count, size = leaf_inv.shape[1], leaf_inv.shape[3]
    width = rhs_leaf.shape[1]
    groups = lax.axis_size("leaf")
    fronts = lax.axis_size("front")

    def stay(value):
        return pltpu.with_memory_space_constraint(value, pltpu.HBM)

    right_leaf, inverse, coupling = stay(rhs_leaf[0]), stay(leaf_inv[0]), stay(leaf_update[0])
    rows = stay(update_rows.reshape(front_count, 1, size))
    owners = stay(update_owner.reshape(front_count))
    separator_inverse, separator_couple = sep_inv[0, 0], sep_couple[0, 0]

    def specs(step):
        matrices = pl.BlockSpec((step, size, size), lambda s: (s, 0, 0))
        lines = pl.BlockSpec((step, 1, size), lambda s: (s, 0, 0))
        vectors = pl.BlockSpec((step, width, size), lambda s: (s, 0, 0))
        columns = pl.BlockSpec((width, step * size), lambda s: (0, s))
        return matrices, lines, vectors, columns

    leaf = lax.axis_index("leaf").reshape(1)
    matrices, lines, vectors, columns = specs(FORWARD_STEP)
    whole = pl.BlockSpec((fronts, width, size), lambda s: (0, 0, 0))
    leaf_y, dense = call(
        leaf_forward,
        [SMEM, SMEM, columns, matrices, matrices, lines],
        [vectors, whole],
        [floats(front_count, width, size), floats(fronts, width, size)],
        grid=(front_count // FORWARD_STEP,),
    )(leaf, owners, right_leaf, inverse, coupling, rows)
    received = exchange(dense, neighbours).reshape(CLASSES, fronts // CLASSES, width, size)
    received = exchange(jnp.sum(received, axis=0), members)

    coupled = call(coupled_inverse, [VMEM, VMEM, ANY], VMEM, floats(1, size, size))(
        separator_inverse, separator_couple, leaf_y
    )
    coupled = gather_by_bits(coupled, "leaf")
    matrices, lines, vectors, columns = specs(PREPARE_STEP)
    mapped = call(
        leaf_prepare,
        [vectors, matrices, matrices, lines],
        pl.BlockSpec((PREPARE_STEP, size + width, 2 * size), lambda s: (s, 0, 0)),
        jax.ShapeDtypeStruct((front_count, size + width, 2 * size), jnp.bfloat16),
        grid=(front_count // PREPARE_STEP,),
    )(leaf_y, inverse, coupling, rows)

    right = call(reduce_right, [VMEM, VMEM, VMEM], VMEM, floats(groups, width, size))(
        received, rhs_sep[0], separator_inverse
    )
    right = lax.all_to_all(right, "leaf", 0, 0, tiled=True)
    x_sep, copies = call(
        chain,
        [SMEM, VMEM, VMEM, VMEM],
        [VMEM, VMEM],
        [floats(width, size), floats(fronts // CLASSES, width, size)],
        scratch_shapes=[pltpu.VMEM((groups, width, size), jnp.float32)],
    )(lax.axis_index("leaf").reshape(1), right, coupled, separator_inverse)
    gathered, mapped = lax.optimization_barrier((exchange(copies, members), mapped))
    gathered = jnp.broadcast_to(gathered[None], (CLASSES, *gathered.shape)).reshape(fronts, width, size)
    gathered = exchange(gathered, neighbours)
    x_leaf = call(
        leaf_backward,
        [SMEM, SMEM, VMEM, VMEM],
        ANY,
        floats(width, front_count * size),
        scratch_shapes=[
            pltpu.VMEM((width, front_count * size), jnp.float32),
            pltpu.SemaphoreType.DMA((front_count // BACKWARD_CHUNK,)),
        ],
    )(leaf, update_owner.reshape(front_count), gathered, mapped)
    return (x_leaf[None], x_sep[None])


def solution(mesh):
    placed = (
        P("leaf", None, "front"),
        P("leaf", None, "front"),
        P("leaf", "front", None, None),
        P("leaf", "front", None, None),
        P("leaf", "front", None),
        P("leaf", "front", None),
        P("leaf", "front", None, None),
        P("leaf", "front", None, None),
    )
    return jax.shard_map(
        per_device,
        mesh=mesh,
        in_specs=placed,
        out_specs=(P("leaf", None, "front"), P("leaf", None, "front")),
        check_vma=False,
    )
```

```python
import jax
import jax.numpy as jnp
from jax import lax
from jax.experimental import pallas as pl
from jax.experimental.pallas import tpu as pltpu
from jax.sharding import PartitionSpec as P

NT = (((1,), (1,)), ((), ()))
NN = (((1,), (0,)), ((), ()))


def dot(left, right, dims):
    return lax.dot_general(left, right, dims, preferred_element_type=jnp.float32)


def split(value):
    high = value.astype(jnp.bfloat16)
    low = (value - high.astype(jnp.float32)).astype(jnp.bfloat16)
    return high, low


def three_parts(parts, rows, size):
    return parts[:rows, :size] + (parts[rows:, :size] + parts[:rows, size:])


def product(left, right, dims):
    along = 0 if dims is NT else 1
    parts = dot(jnp.concatenate(split(left), axis=0), jnp.concatenate(split(right), axis=along), dims)
    return three_parts(parts, left.shape[0], right.shape[0])


def select(left, chosen, dims):
    rows = left.shape[0]
    both = dot(jnp.concatenate(split(left), axis=0), chosen, dims)
    return both[:rows] + both[rows:]


def chosen_rows(row_index, block_rows):
    separator_row = lax.broadcasted_iota(jnp.int32, (block_rows, block_rows), 0)
    return jnp.where(separator_row == row_index, 1.0, 0.0).astype(jnp.bfloat16)


def class_of(index):
    return (index & 1) ^ (index >> (EDGE_BITS - 1))


def slot_of(owner, leaf):
    shift = 2 - (leaf & 1)
    y = ((owner >> EDGE_BITS) - shift) & (EDGE - 1)
    z = (owner - shift) & (EDGE - 1)
    place = ((y >> 1) << (EDGE_BITS - 1)) | (z >> 1)
    return ((class_of(y) << 1) | class_of(z)) * (EDGE * EDGE // CLASSES) + place


def leaf_forward(leaf_ref, owner_ref, rhs_ref, inv_ref, update_ref, rows_ref, y_ref, dense_ref):
    step = pl.program_id(0)
    count, size, _ = inv_ref.shape

    @pl.when(step == 0)
    def _():
        dense_ref[...] = jnp.zeros_like(dense_ref)

    leaf_y = [product(rhs_ref[:, f * size : (f + 1) * size], inv_ref[f], NT) for f in range(count)]
    for f in range(count):
        y_ref[f] = leaf_y[f]
    updates = [product(leaf_y[f], update_ref[f], NT) for f in range(count)]
    placed = [select(updates[f], chosen_rows(rows_ref[f], size), NT) for f in range(count)]
    for f in range(count):
        dense_ref[slot_of(owner_ref[step * count + f], leaf_ref[0])] = placed[f]


def coupled_inverse(inv_ref, couple_ref, after_ref, out_ref):
    out_ref[0] = product(inv_ref[...], couple_ref[...], NN)


def leaf_prepare(y_ref, inv_ref, update_ref, rows_ref, mapped_ref):
    count, size, _ = inv_ref.shape
    fronts = range(count)
    both = [product(jnp.concatenate([update_ref[f], y_ref[f]], axis=0), inv_ref[f], NN) for f in fronts]
    mapped = [jnp.concatenate(split(both[f][:size]), axis=1) for f in fronts]
    for f in fronts:
        mapped_ref[f, size:] = jnp.concatenate(split(both[f][size:]), axis=1)
    placed = [dot(chosen_rows(rows_ref[f], size), mapped[f], NN) for f in fronts]
    for f in fronts:
        whole = placed[f][:, :size] + placed[f][:, size:]
        mapped_ref[f, :size] = jnp.concatenate(split(whole), axis=1)


def reduce_right(received_ref, rhs_ref, inv_ref, out_ref):
    reduced = rhs_ref[...] - jnp.sum(received_ref[...], axis=0)
    solved = product(reduced, inv_ref[...], NT)
    for copy in range(out_ref.shape[0]):
        out_ref[copy] = solved


def chain(group_ref, right_ref, coupled_ref, inv_ref, x_ref, copies_ref, scratch):
    groups = right_ref.shape[0]
    own = group_ref[0]
    solved = [right_ref[0]]
    for group in range(1, groups):
        coupled = coupled_ref[jnp.bitwise_xor(own, group)]
        solved.append(right_ref[group] - product(solved[-1], coupled, NT))
    residue = solved[-1]
    scratch[groups - 1] = residue
    for group in range(groups - 1, 0, -1):
        coupled = coupled_ref[jnp.bitwise_xor(own, group)]
        residue = solved[group - 1] - product(residue, coupled, NN)
        scratch[group - 1] = residue
    x_sep = product(scratch[own], inv_ref[...], NN)
    x_ref[...] = x_sep
    for copy in range(copies_ref.shape[0]):
        copies_ref[copy] = x_sep


def leaf_backward(leaf_ref, owner_ref, x_ref, mapped_ref, out_hbm, out_ref, stored):
    count = mapped_ref.shape[0]
    rows = out_ref.shape[0]
    size = out_ref.shape[1] // count
    stores = []
    for f in range(count):
        owned = jnp.concatenate(split(x_ref[slot_of(owner_ref[f], leaf_ref[0])]), axis=0)
        picked = three_parts(dot(owned, mapped_ref[f, :size], NN), rows, size)
        own = mapped_ref[f, size:].astype(jnp.float32)
        out_ref[:, f * size : (f + 1) * size] = (own[:, :size] + own[:, size:]) - picked
        if (f + 1) % BACKWARD_CHUNK == 0:
            here = slice((f + 1 - BACKWARD_CHUNK) * size, (f + 1) * size)
            store = pltpu.make_async_copy(
                out_ref.at[:, here], out_hbm.at[:, here], stored.at[f // BACKWARD_CHUNK]
            )
            store.start()
            stores.append(store)
    for store in stores:
        store.wait()


EDGE_BITS = 3
EDGE = 1 << EDGE_BITS
CLASSES = 4
BACKWARD_CHUNK = 7
FORWARD_STEP = 14
PREPARE_STEP = 14
VMEM = pl.BlockSpec(memory_space=pltpu.VMEM)
SMEM = pl.BlockSpec(memory_space=pltpu.SMEM)
ANY = pl.BlockSpec(memory_space=pl.ANY)
PARAMS = pltpu.CompilerParams(vmem_limit_bytes=32 << 20)


def floats(*shape):
    return jax.ShapeDtypeStruct(shape, jnp.float32)


def call(body, in_specs, out_specs, out_shape, **rest):
    return pl.pallas_call(
        body,
        in_specs=in_specs,
        out_specs=out_specs,
        out_shape=out_shape,
        compiler_params=PARAMS,
        name=body.__name__,
        **rest,
    )


def exchange(value, groups_of_leaf):
    fronts = lax.axis_size("front")
    groups = [
        [leaf * fronts + front for front in group]
        for leaf in range(lax.axis_size("leaf"))
        for group in groups_of_leaf(leaf)
    ]
    return lax.all_to_all(value, ("leaf", "front"), 0, 0, tiled=True, axis_index_groups=groups)


def device(y, z, leaf):
    shift = 2 - leaf % 2
    return (y + shift) % EDGE * EDGE + (z + shift) % EDGE


def of_class(first, kind):
    return first if class_of(first) == kind else first + 1


def neighbours(leaf):
    kinds = [(a, b) for a in range(2) for b in range(2)]
    pairs = range(0, EDGE, 2)
    return [[device(of_class(y, a), of_class(z, b), leaf) for a, b in kinds] for y in pairs for z in pairs]


def members(leaf):
    kinds = [(a, b) for a in range(2) for b in range(2)]
    pairs = range(0, EDGE, 2)
    return [[device(of_class(y, a), of_class(z, b), leaf) for y in pairs for z in pairs] for a, b in kinds]


def gather_by_bits(value, axis):
    count, bit = lax.axis_size(axis), 1
    while bit < count:
        pairs = [(source, source ^ bit) for source in range(count)]
        value = jnp.concatenate([value, lax.ppermute(value, axis, pairs)], axis=0)
        bit *= 2
    return value


def per_device(
    rhs_leaf, rhs_sep, leaf_inv, leaf_update, update_rows, update_owner, sep_inv, sep_couple
):
    front_count, size = leaf_inv.shape[1], leaf_inv.shape[3]
    width = rhs_leaf.shape[1]
    groups = lax.axis_size("leaf")
    fronts = lax.axis_size("front")

    def stay(value):
        return pltpu.with_memory_space_constraint(value, pltpu.HBM)

    right_leaf, inverse, coupling = stay(rhs_leaf[0]), stay(leaf_inv[0]), stay(leaf_update[0])
    rows = stay(update_rows.reshape(front_count, 1, size))
    owners = stay(update_owner.reshape(front_count))
    separator_inverse, separator_couple = sep_inv[0, 0], sep_couple[0, 0]

    def specs(step):
        matrices = pl.BlockSpec((step, size, size), lambda s: (s, 0, 0))
        lines = pl.BlockSpec((step, 1, size), lambda s: (s, 0, 0))
        vectors = pl.BlockSpec((step, width, size), lambda s: (s, 0, 0))
        columns = pl.BlockSpec((width, step * size), lambda s: (0, s))
        return matrices, lines, vectors, columns

    leaf = lax.axis_index("leaf").reshape(1)
    matrices, lines, vectors, columns = specs(FORWARD_STEP)
    whole = pl.BlockSpec((fronts, width, size), lambda s: (0, 0, 0))
    leaf_y, dense = call(
        leaf_forward,
        [SMEM, SMEM, columns, matrices, matrices, lines],
        [vectors, whole],
        [floats(front_count, width, size), floats(fronts, width, size)],
        grid=(front_count // FORWARD_STEP,),
    )(leaf, owners, right_leaf, inverse, coupling, rows)
    received = exchange(dense, neighbours).reshape(CLASSES, fronts // CLASSES, width, size)
    received = exchange(jnp.sum(received, axis=0), members)

    coupled = call(coupled_inverse, [VMEM, VMEM, ANY], VMEM, floats(1, size, size))(
        separator_inverse, separator_couple, leaf_y
    )
    coupled = gather_by_bits(coupled, "leaf")
    matrices, lines, vectors, columns = specs(PREPARE_STEP)
    mapped = call(
        leaf_prepare,
        [vectors, matrices, matrices, lines],
        pl.BlockSpec((PREPARE_STEP, size + width, 2 * size), lambda s: (s, 0, 0)),
        jax.ShapeDtypeStruct((front_count, size + width, 2 * size), jnp.bfloat16),
        grid=(front_count // PREPARE_STEP,),
    )(leaf_y, inverse, coupling, rows)

    right = call(reduce_right, [VMEM, VMEM, VMEM], VMEM, floats(groups, width, size))(
        received, rhs_sep[0], separator_inverse
    )
    right = lax.all_to_all(right, "leaf", 0, 0, tiled=True)
    x_sep, copies = call(
        chain,
        [SMEM, VMEM, VMEM, VMEM],
        [VMEM, VMEM],
        [floats(width, size), floats(fronts // CLASSES, width, size)],
        scratch_shapes=[pltpu.VMEM((groups, width, size), jnp.float32)],
    )(lax.axis_index("leaf").reshape(1), right, coupled, separator_inverse)
    gathered, mapped = lax.optimization_barrier((exchange(copies, members), mapped))
    gathered = jnp.broadcast_to(gathered[None], (CLASSES, *gathered.shape)).reshape(fronts, width, size)
    gathered = exchange(gathered, neighbours)
    x_leaf = call(
        leaf_backward,
        [SMEM, SMEM, VMEM, VMEM],
        ANY,
        floats(width, front_count * size),
        scratch_shapes=[
            pltpu.VMEM((width, front_count * size), jnp.float32),
            pltpu.SemaphoreType.DMA((front_count // BACKWARD_CHUNK,)),
        ],
    )(leaf, update_owner.reshape(front_count), gathered, mapped)
    return (x_leaf[None], x_sep[None])


def solution(mesh):
    placed = (
        P("leaf", None, "front"),
        P("leaf", None, "front"),
        P("leaf", "front", None, None),
        P("leaf", "front", None, None),
        P("leaf", "front", None),
        P("leaf", "front", None),
        P("leaf", "front", None, None),
        P("leaf", "front", None, None),
    )
    return jax.shard_map(
        per_device,
        mesh=mesh,
        in_specs=placed,
        out_specs=(P("leaf", None, "front"), P("leaf", None, "front")),
        check_vma=False,
    )
```

```python
import jax
import jax.numpy as jnp
from jax import lax
from jax.experimental import pallas as pl
from jax.experimental.pallas import tpu as pltpu
from jax.sharding import PartitionSpec as P

NT = (((1,), (1,)), ((), ()))
NN = (((1,), (0,)), ((), ()))


def dot(left, right, dims):
    return lax.dot_general(left, right, dims, preferred_element_type=jnp.float32)


def split(value):
    high = value.astype(jnp.bfloat16)
    low = (value - high.astype(jnp.float32)).astype(jnp.bfloat16)
    return high, low


def three_parts(parts, rows, size):
    return parts[:rows, :size] + (parts[rows:, :size] + parts[:rows, size:])


def product(left, right, dims):
    along = 0 if dims is NT else 1
    parts = dot(jnp.concatenate(split(left), axis=0), jnp.concatenate(split(right), axis=along), dims)
    return three_parts(parts, left.shape[0], right.shape[0])


def select(left, chosen, dims):
    rows = left.shape[0]
    both = dot(jnp.concatenate(split(left), axis=0), chosen, dims)
    return both[:rows] + both[rows:]


def chosen_rows(row_index, block_rows):
    separator_row = lax.broadcasted_iota(jnp.int32, (block_rows, block_rows), 0)
    return jnp.where(separator_row == row_index, 1.0, 0.0).astype(jnp.bfloat16)


def class_of(index):
    return (index & 1) ^ (index >> (EDGE_BITS - 1))


def slot_of(owner, leaf):
    shift = 3 * (leaf & 1)
    y = ((owner >> EDGE_BITS) - shift) & (EDGE - 1)
    z = (owner - shift) & (EDGE - 1)
    place = ((y >> 1) << (EDGE_BITS - 1)) | (z >> 1)
    return ((class_of(y) << 1) | class_of(z)) * (EDGE * EDGE // CLASSES) + place


def leaf_forward(leaf_ref, owner_ref, rhs_ref, inv_ref, update_ref, rows_ref, y_ref, dense_ref):
    step = pl.program_id(0)
    count, size, _ = inv_ref.shape

    @pl.when(step == 0)
    def _():
        dense_ref[...] = jnp.zeros_like(dense_ref)

    leaf_y = [product(rhs_ref[:, f * size : (f + 1) * size], inv_ref[f], NT) for f in range(count)]
    for f in range(count):
        y_ref[f] = leaf_y[f]
    updates = [product(leaf_y[f], update_ref[f], NT) for f in range(count)]
    placed = [select(updates[f], chosen_rows(rows_ref[f], size), NT) for f in range(count)]
    for f in range(count):
        dense_ref[slot_of(owner_ref[step * count + f], leaf_ref[0])] = placed[f]


def coupled_inverse(inv_ref, couple_ref, after_ref, out_ref):
    out_ref[0] = product(inv_ref[...], couple_ref[...], NN)


def leaf_prepare(y_ref, inv_ref, update_ref, rows_ref, mapped_ref):
    count, size, _ = inv_ref.shape
    fronts = range(count)
    both = [product(jnp.concatenate([update_ref[f], y_ref[f]], axis=0), inv_ref[f], NN) for f in fronts]
    mapped = [jnp.concatenate(split(both[f][:size]), axis=1) for f in fronts]
    for f in fronts:
        mapped_ref[f, size:] = jnp.concatenate(split(both[f][size:]), axis=1)
    placed = [dot(chosen_rows(rows_ref[f], size), mapped[f], NN) for f in fronts]
    for f in fronts:
        whole = placed[f][:, :size] + placed[f][:, size:]
        mapped_ref[f, :size] = jnp.concatenate(split(whole), axis=1)


def reduce_right(received_ref, rhs_ref, inv_ref, out_ref):
    reduced = rhs_ref[...] - jnp.sum(received_ref[...], axis=0)
    solved = product(reduced, inv_ref[...], NT)
    for copy in range(out_ref.shape[0]):
        out_ref[copy] = solved


def chain(group_ref, right_ref, coupled_ref, inv_ref, x_ref, copies_ref, scratch):
    groups = right_ref.shape[0]
    own = group_ref[0]
    solved = [right_ref[0]]
    for group in range(1, groups):
        coupled = coupled_ref[jnp.bitwise_xor(own, group)]
        solved.append(right_ref[group] - product(solved[-1], coupled, NT))
    residue = solved[-1]
    scratch[groups - 1] = residue
    for group in range(groups - 1, 0, -1):
        coupled = coupled_ref[jnp.bitwise_xor(own, group)]
        residue = solved[group - 1] - product(residue, coupled, NN)
        scratch[group - 1] = residue
    x_sep = product(scratch[own], inv_ref[...], NN)
    x_ref[...] = x_sep
    for copy in range(copies_ref.shape[0]):
        copies_ref[copy] = x_sep


def leaf_backward(leaf_ref, owner_ref, x_ref, mapped_ref, out_hbm, out_ref, stored):
    count = mapped_ref.shape[0]
    rows = out_ref.shape[0]
    size = out_ref.shape[1] // count
    stores = []
    for f in range(count):
        owned = jnp.concatenate(split(x_ref[slot_of(owner_ref[f], leaf_ref[0])]), axis=0)
        picked = three_parts(dot(owned, mapped_ref[f, :size], NN), rows, size)
        own = mapped_ref[f, size:].astype(jnp.float32)
        out_ref[:, f * size : (f + 1) * size] = (own[:, :size] + own[:, size:]) - picked
        if (f + 1) % BACKWARD_CHUNK == 0:
            here = slice((f + 1 - BACKWARD_CHUNK) * size, (f + 1) * size)
            store = pltpu.make_async_copy(
                out_ref.at[:, here], out_hbm.at[:, here], stored.at[f // BACKWARD_CHUNK]
            )
            store.start()
            stores.append(store)
    for store in stores:
        store.wait()


EDGE_BITS = 3
EDGE = 1 << EDGE_BITS
CLASSES = 4
BACKWARD_CHUNK = 7
FORWARD_STEP = 14
PREPARE_STEP = 14
VMEM = pl.BlockSpec(memory_space=pltpu.VMEM)
SMEM = pl.BlockSpec(memory_space=pltpu.SMEM)
ANY = pl.BlockSpec(memory_space=pl.ANY)
PARAMS = pltpu.CompilerParams(vmem_limit_bytes=32 << 20)


def floats(*shape):
    return jax.ShapeDtypeStruct(shape, jnp.float32)


def call(body, in_specs, out_specs, out_shape, **rest):
    return pl.pallas_call(
        body,
        in_specs=in_specs,
        out_specs=out_specs,
        out_shape=out_shape,
        compiler_params=PARAMS,
        name=body.__name__,
        **rest,
    )


def exchange(value, groups_of_leaf):
    fronts = lax.axis_size("front")
    groups = [
        [leaf * fronts + front for front in group]
        for leaf in range(lax.axis_size("leaf"))
        for group in groups_of_leaf(leaf)
    ]
    return lax.all_to_all(value, ("leaf", "front"), 0, 0, tiled=True, axis_index_groups=groups)


def device(y, z, leaf):
    shift = 3 * (leaf % 2)
    return (y + shift) % EDGE * EDGE + (z + shift) % EDGE


def of_class(first, kind):
    return first if class_of(first) == kind else first + 1


def neighbours(leaf):
    kinds = [(a, b) for a in range(2) for b in range(2)]
    pairs = range(0, EDGE, 2)
    return [[device(of_class(y, a), of_class(z, b), leaf) for a, b in kinds] for y in pairs for z in pairs]


def members(leaf):
    kinds = [(a, b) for a in range(2) for b in range(2)]
    pairs = range(0, EDGE, 2)
    return [[device(of_class(y, a), of_class(z, b), leaf) for y in pairs for z in pairs] for a, b in kinds]


def gather_by_bits(value, axis):
    count, bit = lax.axis_size(axis), 1
    while bit < count:
        pairs = [(source, source ^ bit) for source in range(count)]
        value = jnp.concatenate([value, lax.ppermute(value, axis, pairs)], axis=0)
        bit *= 2
    return value


def per_device(
    rhs_leaf, rhs_sep, leaf_inv, leaf_update, update_rows, update_owner, sep_inv, sep_couple
):
    front_count, size = leaf_inv.shape[1], leaf_inv.shape[3]
    width = rhs_leaf.shape[1]
    groups = lax.axis_size("leaf")
    fronts = lax.axis_size("front")

    def stay(value):
        return pltpu.with_memory_space_constraint(value, pltpu.HBM)

    right_leaf, inverse, coupling = stay(rhs_leaf[0]), stay(leaf_inv[0]), stay(leaf_update[0])
    rows = stay(update_rows.reshape(front_count, 1, size))
    owners = stay(update_owner.reshape(front_count))
    separator_inverse, separator_couple = sep_inv[0, 0], sep_couple[0, 0]

    def specs(step):
        matrices = pl.BlockSpec((step, size, size), lambda s: (s, 0, 0))
        lines = pl.BlockSpec((step, 1, size), lambda s: (s, 0, 0))
        vectors = pl.BlockSpec((step, width, size), lambda s: (s, 0, 0))
        columns = pl.BlockSpec((width, step * size), lambda s: (0, s))
        return matrices, lines, vectors, columns

    leaf = lax.axis_index("leaf").reshape(1)
    matrices, lines, vectors, columns = specs(FORWARD_STEP)
    whole = pl.BlockSpec((fronts, width, size), lambda s: (0, 0, 0))
    leaf_y, dense = call(
        leaf_forward,
        [SMEM, SMEM, columns, matrices, matrices, lines],
        [vectors, whole],
        [floats(front_count, width, size), floats(fronts, width, size)],
        grid=(front_count // FORWARD_STEP,),
    )(leaf, owners, right_leaf, inverse, coupling, rows)
    received = exchange(dense, neighbours).reshape(CLASSES, fronts // CLASSES, width, size)
    received = exchange(jnp.sum(received, axis=0), members)

    coupled = call(coupled_inverse, [VMEM, VMEM, ANY], VMEM, floats(1, size, size))(
        separator_inverse, separator_couple, leaf_y
    )
    coupled = gather_by_bits(coupled, "leaf")
    matrices, lines, vectors, columns = specs(PREPARE_STEP)
    mapped = call(
        leaf_prepare,
        [vectors, matrices, matrices, lines],
        pl.BlockSpec((PREPARE_STEP, size + width, 2 * size), lambda s: (s, 0, 0)),
        jax.ShapeDtypeStruct((front_count, size + width, 2 * size), jnp.bfloat16),
        grid=(front_count // PREPARE_STEP,),
    )(leaf_y, inverse, coupling, rows)

    right = call(reduce_right, [VMEM, VMEM, VMEM], VMEM, floats(groups, width, size))(
        received, rhs_sep[0], separator_inverse
    )
    right = lax.all_to_all(right, "leaf", 0, 0, tiled=True)
    x_sep, copies = call(
        chain,
        [SMEM, VMEM, VMEM, VMEM],
        [VMEM, VMEM],
        [floats(width, size), floats(fronts // CLASSES, width, size)],
        scratch_shapes=[pltpu.VMEM((groups, width, size), jnp.float32)],
    )(lax.axis_index("leaf").reshape(1), right, coupled, separator_inverse)
    gathered, mapped = lax.optimization_barrier((exchange(copies, members), mapped))
    gathered = jnp.broadcast_to(gathered[None], (CLASSES, *gathered.shape)).reshape(fronts, width, size)
    gathered = exchange(gathered, neighbours)
    x_leaf = call(
        leaf_backward,
        [SMEM, SMEM, VMEM, VMEM],
        ANY,
        floats(width, front_count * size),
        scratch_shapes=[
            pltpu.VMEM((width, front_count * size), jnp.float32),
            pltpu.SemaphoreType.DMA((front_count // BACKWARD_CHUNK,)),
        ],
    )(leaf, update_owner.reshape(front_count), gathered, mapped)
    return (x_leaf[None], x_sep[None])


def solution(mesh):
    placed = (
        P("leaf", None, "front"),
        P("leaf", None, "front"),
        P("leaf", "front", None, None),
        P("leaf", "front", None, None),
        P("leaf", "front", None),
        P("leaf", "front", None),
        P("leaf", "front", None, None),
        P("leaf", "front", None, None),
    )
    return jax.shard_map(
        per_device,
        mesh=mesh,
        in_specs=placed,
        out_specs=(P("leaf", None, "front"), P("leaf", None, "front")),
        check_vma=False,
    )
```

```python
import jax
import jax.numpy as jnp
from jax import lax
from jax.experimental import pallas as pl
from jax.experimental.pallas import tpu as pltpu
from jax.sharding import PartitionSpec as P

NT = (((1,), (1,)), ((), ()))
NN = (((1,), (0,)), ((), ()))


def dot(left, right, dims):
    return lax.dot_general(left, right, dims, preferred_element_type=jnp.float32)


def split(value):
    high = value.astype(jnp.bfloat16)
    low = (value - high.astype(jnp.float32)).astype(jnp.bfloat16)
    return high, low


def three_parts(parts, rows, size):
    return parts[:rows, :size] + (parts[rows:, :size] + parts[:rows, size:])


def product(left, right, dims):
    along = 0 if dims is NT else 1
    parts = dot(jnp.concatenate(split(left), axis=0), jnp.concatenate(split(right), axis=along), dims)
    return three_parts(parts, left.shape[0], right.shape[0])


def select(left, chosen, dims):
    rows = left.shape[0]
    both = dot(jnp.concatenate(split(left), axis=0), chosen, dims)
    return both[:rows] + both[rows:]


def chosen_rows(row_index, block_rows):
    separator_row = lax.broadcasted_iota(jnp.int32, (block_rows, block_rows), 0)
    return jnp.where(separator_row == row_index, 1.0, 0.0).astype(jnp.bfloat16)


def class_of(index):
    return (index & 1) ^ (index >> (EDGE_BITS - 1))


def slot_of(owner, leaf):
    y = ((owner >> EDGE_BITS) - (leaf & 1)) & (EDGE - 1)
    z = (owner - (leaf & 1)) & (EDGE - 1)
    place = ((y >> 1) << (EDGE_BITS - 1)) | (z >> 1)
    return ((class_of(y) << 1) | class_of(z)) * (EDGE * EDGE // CLASSES) + place


def leaf_forward(leaf_ref, owner_ref, rhs_ref, inv_ref, update_ref, rows_ref, y_ref, dense_ref):
    step = pl.program_id(0)
    count, size, _ = inv_ref.shape

    @pl.when(step == 0)
    def _():
        dense_ref[...] = jnp.zeros_like(dense_ref)

    leaf_y = [product(rhs_ref[:, f * size : (f + 1) * size], inv_ref[f], NT) for f in range(count)]
    for f in range(count):
        y_ref[f] = leaf_y[f]
    updates = [product(leaf_y[f], update_ref[f], NT) for f in range(count)]
    placed = [select(updates[f], chosen_rows(rows_ref[f], size), NT) for f in range(count)]
    for f in range(count):
        dense_ref[slot_of(owner_ref[step * count + f], leaf_ref[0])] = placed[f]


def coupled_inverse(inv_ref, couple_ref, after_ref, out_ref):
    out_ref[0] = product(inv_ref[...], couple_ref[...], NN)


def leaf_prepare(y_ref, inv_ref, update_ref, rows_ref, mapped_ref):
    count, size, _ = inv_ref.shape
    fronts = range(count)
    both = [product(jnp.concatenate([update_ref[f], y_ref[f]], axis=0), inv_ref[f], NN) for f in fronts]
    mapped = [jnp.concatenate(split(both[f][:size]), axis=1) for f in fronts]
    for f in fronts:
        mapped_ref[f, size:] = jnp.concatenate(split(both[f][size:]), axis=1)
    placed = [dot(chosen_rows(rows_ref[f], size), mapped[f], NN) for f in fronts]
    for f in fronts:
        whole = placed[f][:, :size] + placed[f][:, size:]
        mapped_ref[f, :size] = jnp.concatenate(split(whole), axis=1)


def reduce_right(received_ref, rhs_ref, inv_ref, out_ref):
    reduced = rhs_ref[...] - jnp.sum(received_ref[...], axis=0)
    solved = product(reduced, inv_ref[...], NT)
    for copy in range(out_ref.shape[0]):
        out_ref[copy] = solved


def chain(group_ref, right_ref, coupled_ref, inv_ref, x_ref, copies_ref, scratch):
    groups = right_ref.shape[0]
    own = group_ref[0]
    solved = [right_ref[0]]
    for group in range(1, groups):
        coupled = coupled_ref[jnp.bitwise_xor(own, group)]
        solved.append(right_ref[group] - product(solved[-1], coupled, NT))
    residue = solved[-1]
    scratch[groups - 1] = residue
    for group in range(groups - 1, 0, -1):
        coupled = coupled_ref[jnp.bitwise_xor(own, group)]
        residue = solved[group - 1] - product(residue, coupled, NN)
        scratch[group - 1] = residue
    x_sep = product(scratch[own], inv_ref[...], NN)
    x_ref[...] = x_sep
    for copy in range(copies_ref.shape[0]):
        copies_ref[copy] = x_sep


def leaf_backward(leaf_ref, owner_ref, x_ref, mapped_ref, out_hbm, out_ref, stored):
    count = mapped_ref.shape[0]
    rows = out_ref.shape[0]
    size = out_ref.shape[1] // count
    stores = []
    for first in range(0, count, BACKWARD_CHUNK):
        chunk = range(first, first + BACKWARD_CHUNK)
        owned = [jnp.concatenate(split(x_ref[slot_of(owner_ref[f], leaf_ref[0])]), axis=0) for f in chunk]
        parts = [dot(value, mapped_ref[f, :size], NN) for f, value in zip(chunk, owned)]
        for f, part in zip(chunk, parts):
            own = mapped_ref[f, size:].astype(jnp.float32)
            own = own[:, :size] + own[:, size:]
            out_ref[:, f * size : (f + 1) * size] = own - three_parts(part, rows, size)
        here = slice(first * size, (first + BACKWARD_CHUNK) * size)
        store = pltpu.make_async_copy(
            out_ref.at[:, here], out_hbm.at[:, here], stored.at[first // BACKWARD_CHUNK]
        )
        store.start()
        stores.append(store)
    for store in stores:
        store.wait()


EDGE_BITS = 3
EDGE = 1 << EDGE_BITS
CLASSES = 4
BACKWARD_CHUNK = 7
FORWARD_STEP = 14
PREPARE_STEP = 14
VMEM = pl.BlockSpec(memory_space=pltpu.VMEM)
SMEM = pl.BlockSpec(memory_space=pltpu.SMEM)
ANY = pl.BlockSpec(memory_space=pl.ANY)
PARAMS = pltpu.CompilerParams(vmem_limit_bytes=32 << 20)


def floats(*shape):
    return jax.ShapeDtypeStruct(shape, jnp.float32)


def call(body, in_specs, out_specs, out_shape, **rest):
    return pl.pallas_call(
        body,
        in_specs=in_specs,
        out_specs=out_specs,
        out_shape=out_shape,
        compiler_params=PARAMS,
        name=body.__name__,
        **rest,
    )


def exchange(value, groups_of_leaf):
    fronts = lax.axis_size("front")
    groups = [
        [leaf * fronts + front for front in group]
        for leaf in range(lax.axis_size("leaf"))
        for group in groups_of_leaf(leaf)
    ]
    return lax.all_to_all(value, ("leaf", "front"), 0, 0, tiled=True, axis_index_groups=groups)


def device(y, z, leaf):
    return (y + leaf % 2) % EDGE * EDGE + (z + leaf % 2) % EDGE


def of_class(first, kind):
    return first if class_of(first) == kind else first + 1


def neighbours(leaf):
    kinds = [(a, b) for a in range(2) for b in range(2)]
    pairs = range(0, EDGE, 2)
    return [[device(of_class(y, a), of_class(z, b), leaf) for a, b in kinds] for y in pairs for z in pairs]


def members(leaf):
    kinds = [(a, b) for a in range(2) for b in range(2)]
    pairs = range(0, EDGE, 2)
    return [[device(of_class(y, a), of_class(z, b), leaf) for y in pairs for z in pairs] for a, b in kinds]


def gather_by_bits(value, axis):
    count, bit = lax.axis_size(axis), 1
    while bit < count:
        pairs = [(source, source ^ bit) for source in range(count)]
        value = jnp.concatenate([value, lax.ppermute(value, axis, pairs)], axis=0)
        bit *= 2
    return value


def per_device(
    rhs_leaf, rhs_sep, leaf_inv, leaf_update, update_rows, update_owner, sep_inv, sep_couple
):
    front_count, size = leaf_inv.shape[1], leaf_inv.shape[3]
    width = rhs_leaf.shape[1]
    groups = lax.axis_size("leaf")
    fronts = lax.axis_size("front")

    def stay(value):
        return pltpu.with_memory_space_constraint(value, pltpu.HBM)

    right_leaf, inverse, coupling = stay(rhs_leaf[0]), stay(leaf_inv[0]), stay(leaf_update[0])
    rows = stay(update_rows.reshape(front_count, 1, size))
    owners = stay(update_owner.reshape(front_count))
    separator_inverse, separator_couple = sep_inv[0, 0], sep_couple[0, 0]

    def specs(step):
        matrices = pl.BlockSpec((step, size, size), lambda s: (s, 0, 0))
        lines = pl.BlockSpec((step, 1, size), lambda s: (s, 0, 0))
        vectors = pl.BlockSpec((step, width, size), lambda s: (s, 0, 0))
        columns = pl.BlockSpec((width, step * size), lambda s: (0, s))
        return matrices, lines, vectors, columns

    leaf = lax.axis_index("leaf").reshape(1)
    matrices, lines, vectors, columns = specs(FORWARD_STEP)
    whole = pl.BlockSpec((fronts, width, size), lambda s: (0, 0, 0))
    leaf_y, dense = call(
        leaf_forward,
        [SMEM, SMEM, columns, matrices, matrices, lines],
        [vectors, whole],
        [floats(front_count, width, size), floats(fronts, width, size)],
        grid=(front_count // FORWARD_STEP,),
    )(leaf, owners, right_leaf, inverse, coupling, rows)
    received = exchange(dense, neighbours).reshape(CLASSES, fronts // CLASSES, width, size)
    received = exchange(jnp.sum(received, axis=0), members)

    coupled = call(coupled_inverse, [VMEM, VMEM, ANY], VMEM, floats(1, size, size))(
        separator_inverse, separator_couple, leaf_y
    )
    coupled = gather_by_bits(coupled, "leaf")
    matrices, lines, vectors, columns = specs(PREPARE_STEP)
    mapped = call(
        leaf_prepare,
        [vectors, matrices, matrices, lines],
        pl.BlockSpec((PREPARE_STEP, size + width, 2 * size), lambda s: (s, 0, 0)),
        jax.ShapeDtypeStruct((front_count, size + width, 2 * size), jnp.bfloat16),
        grid=(front_count // PREPARE_STEP,),
    )(leaf_y, inverse, coupling, rows)

    right = call(reduce_right, [VMEM, VMEM, VMEM], VMEM, floats(groups, width, size))(
        received, rhs_sep[0], separator_inverse
    )
    right = lax.all_to_all(right, "leaf", 0, 0, tiled=True)
    x_sep, copies = call(
        chain,
        [SMEM, VMEM, VMEM, VMEM],
        [VMEM, VMEM],
        [floats(width, size), floats(fronts // CLASSES, width, size)],
        scratch_shapes=[pltpu.VMEM((groups, width, size), jnp.float32)],
    )(lax.axis_index("leaf").reshape(1), right, coupled, separator_inverse)
    gathered, mapped = lax.optimization_barrier((exchange(copies, members), mapped))
    gathered = jnp.broadcast_to(gathered[None], (CLASSES, *gathered.shape)).reshape(fronts, width, size)
    gathered = exchange(gathered, neighbours)
    x_leaf = call(
        leaf_backward,
        [SMEM, SMEM, VMEM, VMEM],
        ANY,
        floats(width, front_count * size),
        scratch_shapes=[
            pltpu.VMEM((width, front_count * size), jnp.float32),
            pltpu.SemaphoreType.DMA((front_count // BACKWARD_CHUNK,)),
        ],
    )(leaf, update_owner.reshape(front_count), gathered, mapped)
    return (x_leaf[None], x_sep[None])


def solution(mesh):
    placed = (
        P("leaf", None, "front"),
        P("leaf", None, "front"),
        P("leaf", "front", None, None),
        P("leaf", "front", None, None),
        P("leaf", "front", None),
        P("leaf", "front", None),
        P("leaf", "front", None, None),
        P("leaf", "front", None, None),
    )
    return jax.shard_map(
        per_device,
        mesh=mesh,
        in_specs=placed,
        out_specs=(P("leaf", None, "front"), P("leaf", None, "front")),
        check_vma=False,
    )
```
